512 devices in a mesh: grp: 16 (over y_lo, x, core), ep: 32 (over z, y_hi).
Axes of the slice: x: 4, y: 4 (y_hi: 2, y_lo: 2; y = y_hi * 2 + y_lo), z: 16, core: 2. Of those that a mesh axis runs over, the one named last changes fastest.
Arguments:
- tokens: bfloat16 [16, 512, 5120], P('grp', 'ep'), may hold values from -6 to 6
- cotangent: bfloat16 [16, 512, 5120], P('grp', 'ep'), may hold values from -1.5 to 1.5
- counts: int32 [16, 32, 4], P('grp', 'ep'), may hold values from 0 to 4, as said below
- destination: int32 [16, 32, 16], P('grp', 'ep'), may hold values from 0 to 15, each once within a row
- placement: int32 [32], replicated, may hold values from 0 to 31, each once
- gate_up_weight: bfloat16 [32, 2, 5120, 128], P('ep', None, 'grp'), may hold values from -0.078125 to 0.078125
- down_weight: bfloat16 [32, 5120, 128], P('ep', 'grp'), may hold values from -0.1875 to 0.1875
Outputs:
- layer_out: bfloat16 [16, 512, 5120], P('grp', 'ep')
- input_grad: bfloat16 [16, 512, 5120], P('grp', 'ep')
- gate_up_grad: float32 [32, 2, 5120, 128], P('ep', None, 'grp')
- down_grad: float32 [32, 5120, 128], P('ep', 'grp')
The draws below stay inside these ranges and needn't reach their ends.
Inputs may be any that keep to these rules, and one draw needn't show every extreme that they name: counts[g, j, e] is the number of kept slots of expert e on device (g, j) after reassignment; some device has all 4 slots of an expert kept in every draw. `destination`: the 16 blocks of one device go to 16 different groups. `placement`: each expert slice is served by exactly one owner.
All inputs are finite; a program needn't handle non-finite values.
Results may differ from the reference program's by a relative error of at most 0.017.
Values may be sent and summed in bfloat16 or wider, within the bound.
No kernel may reach another device: no remote copies, remote signals or barrier semaphores. Data moves between devices by JAX's collectives and lax.ppermute only.
A program may use at most 64 MiB of HBM per device.

```python
import jax
import jax.numpy as jnp
from jax import lax

D = 5120
SLICE = 128
SPLIT = 8
CAP = 4
HID = 1024
EXP_G = 4
TOK_DEV = 16
GROUPS = 16
OWNERS = 32
N_GRP = 16
N_EP = 32


def draw_counts(key, part):
    drawn = jax.random.randint(key, (GROUPS, OWNERS, EXP_G), 0, CAP + 1)
    return drawn.at[0, 0, 0].set(CAP).astype(jnp.int32)


def block_scale(key, dims, shards, smallest, high):
    level, own = 1.0, jax.random.fold_in(key, 6)
    for axis_at, parts in shards:
        heights = jnp.exp(jax.random.uniform(jax.random.fold_in(own, axis_at), (parts,), jnp.float32, smallest / len(shards), high / len(shards)))
        level = level * jnp.repeat(heights, dims[axis_at] // parts).reshape([-1 if axis == axis_at else 1 for axis in range(len(dims))])
    return level


def gaussian(stream_key, dims, scale, bound, cuts=(), kind=jnp.bfloat16):
    values = jax.random.normal(stream_key, dims, jnp.float32) * scale
    if len(cuts) > 0:
        values = block_scale(stream_key, dims, cuts, -0.22, 0.18) * values
    return jnp.clip(values, min=-bound, max=bound).astype(kind)


def setup_inputs(seed: int = 0) -> dict:
    key_list = jax.random.split(jax.random.key(seed), 8)
    tokens = gaussian(key_list[0], (GROUPS, OWNERS * TOK_DEV, D), 1.0, 6.0, ((0, 16), (1, 32)))
    cotangent = gaussian(key_list[1], (GROUPS, OWNERS * TOK_DEV, D), 0.25, 1.5, ((0, 16), (1, 32)))
    counts = draw_counts(jax.random.fold_in(key_list[7], 71), 0)
    destination = jax.vmap(lambda own: jax.random.permutation(own, GROUPS))(jax.random.split(key_list[3], GROUPS * OWNERS)).reshape((GROUPS, OWNERS, GROUPS)).astype(jnp.int32)
    placement = jax.random.permutation(key_list[4], OWNERS).astype(jnp.int32)
    gate_up_weight = gaussian(key_list[5], (OWNERS, 2, D, SLICE), D ** -0.5, 0.078125, ((0, 32), (2, 16)))
    down_weight = gaussian(key_list[6], (OWNERS, D, SLICE), HID ** -0.5, 0.1875, ((0, 32), (1, 16)))
    return dict(tokens=tokens, cotangent=cotangent, counts=counts, destination=destination, placement=placement, gate_up_weight=gate_up_weight, down_weight=down_weight)


def swiglu_backward(gate_up, hidden_grad):
    gate_part = gate_up[0]
    up_part = gate_up[1]
    sigmoid_gate = jax.nn.sigmoid(gate_part)
    activated = gate_part * sigmoid_gate
    hidden = (activated * up_part).astype(jnp.bfloat16)
    gate_grad = hidden_grad * up_part * sigmoid_gate * (1.0 + gate_part * (1.0 - sigmoid_gate))
    up_grad = hidden_grad * activated
    return hidden, jnp.stack([gate_grad, up_grad]).astype(jnp.bfloat16)


def widen(value):
    return lax.optimization_barrier(value).astype(jnp.float32)


def reference(tokens, cotangent, counts, destination, placement, gate_up_weight, down_weight):
    groups = N_GRP
    owners = N_EP
    experts = EXP_G
    capacity = CAP
    block_rows = TOK_DEV // groups
    order = jnp.argsort(destination, axis=-1).astype(jnp.int32)
    group_ids = jnp.arange(groups, dtype=jnp.int32)[:, None, None]
    owner_ids = jnp.arange(owners, dtype=jnp.int32)[None, :, None]
    slot_ids = jnp.arange(capacity, dtype=jnp.int32)[None, None, None, :]
    keep = (slot_ids < counts[:, :, :, None])[..., None]

    def rebalance(full):
        blocks = full.reshape(groups, owners, groups, block_rows, D)
        moved = blocks[group_ids, owner_ids, order]
        moved = jnp.transpose(moved, (2, 1, 0, 3, 4)).reshape(groups, owners, experts, capacity, D)
        return jnp.where(keep, moved, jnp.zeros((), moved.dtype))

    kept_tokens = rebalance(tokens)
    kept_cotangent = rebalance(cotangent)
    expert_of = (placement // SPLIT).astype(jnp.int32)
    owner_table = (expert_of[:, None] == jnp.arange(experts, dtype=jnp.int32)[None, :]).astype(jnp.float32)
    gate_up_full = gate_up_weight.astype(jnp.float32)
    down_full = down_weight.astype(jnp.float32)

    def per_group(carry, pair):
        here_tokens, here_cotangent = pair
        slot_tokens = jnp.transpose(jnp.take(here_tokens, expert_of, axis=1), (1, 0, 2, 3))
        slot_tokens = slot_tokens.reshape(owners, owners * capacity, D).astype(jnp.float32)
        slot_cotangent = jnp.transpose(jnp.take(here_cotangent, expert_of, axis=1), (1, 0, 2, 3))
        slot_cotangent = slot_cotangent.reshape(owners, owners * capacity, D).astype(jnp.float32)
        gate_up = jnp.einsum("jrd,jkds->jkrs", slot_tokens, gate_up_full)
        hidden_grad = jnp.einsum("jrd,jds->jrs", slot_cotangent, down_full)
        hidden, grad_rows = jax.vmap(swiglu_backward)(gate_up, hidden_grad)
        hidden_wide = hidden.astype(jnp.float32)
        grad_wide = grad_rows.astype(jnp.float32)
        forward_part = jnp.einsum("jrs,jds->jrd", hidden_wide, down_full).astype(jnp.bfloat16)
        backward_part = jnp.einsum("jkrs,jkds->jrd", grad_wide, gate_up_full).astype(jnp.bfloat16)
        forward_part = widen(forward_part).reshape(owners, owners, capacity, D)
        backward_part = widen(backward_part).reshape(owners, owners, capacity, D)
        layer_rows = jnp.einsum("jkcd,je->kecd", forward_part, owner_table).astype(jnp.bfloat16)
        grad_rows_out = jnp.einsum("jkcd,je->kecd", backward_part, owner_table).astype(jnp.bfloat16)
        gate_up_term = jnp.einsum("jrd,jkrs->jkds", slot_tokens, grad_wide).astype(jnp.bfloat16)
        down_term = jnp.einsum("jrd,jrs->jds", slot_cotangent, hidden_wide).astype(jnp.bfloat16)
        gate_up_sum = carry[0] + widen(gate_up_term)
        down_sum = carry[1] + widen(down_term)
        outputs = (layer_rows.reshape(owners, TOK_DEV, D), grad_rows_out.reshape(owners, TOK_DEV, D))
        return (gate_up_sum, down_sum), outputs

    initial = (jnp.zeros((owners, 2, D, SLICE), jnp.float32), jnp.zeros((owners, D, SLICE), jnp.float32))
    sums, stacked = lax.scan(per_group, initial, (kept_tokens, kept_cotangent))
    layer_out = stacked[0].reshape(groups, owners * TOK_DEV, D)
    input_grad = stacked[1].reshape(groups, owners * TOK_DEV, D)
    return (layer_out, input_grad, sums[0], sums[1])
```

```python
import functools

import jax
import jax.numpy as jnp
from jax import lax
from jax.experimental import pallas as pl
from jax.experimental.pallas import tpu as pltpu
from jax.sharding import Mesh, PartitionSpec as P

AXES = ("y_lo", "x", "core", "z", "y_hi")
SIZES = (2, 4, 2, 16, 2)
GRP = ("y_lo", "x", "core")
EP = ("z", "y_hi")
PLANE = ("y_hi", "y_lo", "x", "core")

G = 16
Z = 16
Y = 2
E = 4
C = 4
D = 5120
W = D // G
WP = 384
S = 128
R = Y * C * G
BF = jnp.bfloat16
F32 = jnp.float32


def dot(a, b, dims=((1,), (0,))):
    return lax.dot_general(a, b, (dims, ((), ())), preferred_element_type=F32)


def pack_kernel(me_ref, counts_ref, dest_ref, tok_ref, cot_ref, out_ref):
    me = me_ref[0]
    rows = lax.broadcasted_iota(jnp.int32, (G, G), 0)
    pick = (rows == dest_ref[...]).astype(F32).astype(BF)
    lane = lax.broadcasted_iota(jnp.int32, (G, WP), 1)
    row = lax.broadcasted_iota(jnp.int32, (G, WP), 0)
    extra = jnp.zeros((G, WP), F32)
    for e in range(E):
        extra = jnp.where((lane == W + e) & (row == me), counts_ref[e].astype(F32), extra)
    for d in range(G):
        start = d * W // 128 * 128
        for t, ref in enumerate((tok_ref, cot_ref)):
            moved = dot(pick, ref[:, start : start + WP])
            if start != d * W:
                moved = pltpu.roll(moved, WP - (d * W - start), 1)
            moved = jnp.where(lane < W, moved, extra).astype(BF)
            for y in range(Y):
                out_ref[y * G + d, t * G : (t + 1) * G, :] = moved


def pack(me, counts, dest, tokens, cotangent):
    vmem = pl.BlockSpec(memory_space=pltpu.VMEM)
    smem = pl.BlockSpec(memory_space=pltpu.SMEM)
    return pl.pallas_call(
        pack_kernel,
        out_shape=jax.ShapeDtypeStruct((Y * G, 2 * G, WP), BF),
        in_specs=[smem, smem, vmem, vmem, vmem],
        out_specs=vmem,
        name="pack",
    )(me, counts, dest, tokens, cotangent)


def load_rows(recv_ref, x_ref):
    lane = lax.broadcasted_iota(jnp.int32, (G, 128), 1)
    for y in range(Y):
        table = jnp.zeros((G, 128), F32)
        for g in range(G):
            table = table + recv_ref[y * G + g, 0:G, WP - 128 : WP].astype(F32)
        for e in range(E):
            kept = jnp.sum(jnp.where(lane == 128 - (WP - W) + e, table, 0.0), axis=1, keepdims=True)
            for c in range(C):
                keep = jnp.broadcast_to(kept, (G, W)) > c + 0.5
                at = (y * C + c) * G
                for t in range(2):
                    block = recv_ref[y * G + e * C + c, t * G : (t + 1) * G, 0:W].astype(F32)
                    x_ref[t, e, at : at + G, :] = jnp.where(keep, block, 0.0).astype(BF)


def first_kernel(expert_ref, recv_ref, weight_ref, out_ref, x_ref):
    load_rows(recv_ref, x_ref)

    def step(z, carry):
        e = expert_ref[z]
        tok = x_ref[0, e]
        cot = x_ref[1, e]
        out_ref[z, :, 0:S] = dot(tok, weight_ref[z, 0]).astype(BF)
        out_ref[z, :, S : 2 * S] = dot(tok, weight_ref[z, 1]).astype(BF)
        out_ref[z, :, 2 * S : 3 * S] = dot(cot, weight_ref[z, 2]).astype(BF)
        return carry

    lax.fori_loop(0, Z, step, 0)


def first(expert, recv, weight):
    vmem = pl.BlockSpec(memory_space=pltpu.VMEM)
    smem = pl.BlockSpec(memory_space=pltpu.SMEM)
    return pl.pallas_call(
        first_kernel,
        out_shape=jax.ShapeDtypeStruct((Z, R, 3 * S), BF),
        in_specs=[smem, vmem, vmem],
        out_specs=vmem,
        scratch_shapes=[pltpu.VMEM((2, E, R, W), BF)],
        name="first",
    )(expert, recv, weight)


def middle_kernel(part_ref, out_ref):
    total = part_ref[0].astype(F32)
    for d in range(1, G):
        total = total + part_ref[d].astype(F32)
    gate = total[:, 0:S]
    up = total[:, S : 2 * S]
    hidden_grad = total[:, 2 * S : 3 * S]
    sigmoid = jax.nn.sigmoid(gate)
    activated = gate * sigmoid
    out_ref[:, 0:S] = (activated * up).astype(BF)
    grad = hidden_grad * up * sigmoid * (1.0 + gate * (1.0 - sigmoid))
    out_ref[:, S : 2 * S] = grad.astype(BF)
    out_ref[:, 2 * S : 3 * S] = (hidden_grad * activated).astype(BF)


def middle(parts):
    vmem = pl.BlockSpec(memory_space=pltpu.VMEM)
    return pl.pallas_call(
        middle_kernel,
        out_shape=jax.ShapeDtypeStruct((R, 3 * S), BF),
        in_specs=[vmem],
        out_specs=vmem,
        name="middle",
    )(parts)


def last_kernel(expert_ref, recv_ref, weight_ref, act_ref, out_ref, grad_ref, x_ref, acc_ref):
    load_rows(recv_ref, x_ref)
    acc_ref[...] = jnp.zeros_like(acc_ref)
    tail = ((1,), (1,))
    head = ((0,), (0,))

    def step(z, carry):
        e = expert_ref[z]
        hidden = act_ref[z, :, 0:S]
        gate_grad = act_ref[z, :, S : 2 * S]
        up_grad = act_ref[z, :, 2 * S : 3 * S]
        acc_ref[0, e] += dot(hidden, weight_ref[z, 2], tail)
        acc_ref[1, e] += dot(gate_grad, weight_ref[z, 0], tail) + dot(up_grad, weight_ref[z, 1], tail)
        tok = x_ref[0, e]
        cot = x_ref[1, e]
        grad_ref[z, 0] = dot(tok, gate_grad, head).astype(BF)
        grad_ref[z, 1] = dot(tok, up_grad, head).astype(BF)
        grad_ref[z, 2] = dot(cot, hidden, head).astype(BF)
        return carry

    lax.fori_loop(0, Z, step, 0)
    n = E * C * G
    i = lax.broadcasted_iota(jnp.int32, (n, n), 0)
    j = lax.broadcasted_iota(jnp.int32, (n, n), 1)
    swap = ((i // (E * C) == j % G) & (i % (E * C) == j // G)).astype(F32).astype(BF)
    for y in range(Y):
        for t in range(2):
            rows = jnp.concatenate(
                [acc_ref[t, e, y * C * G : (y + 1) * C * G, :].astype(BF) for e in range(E)], axis=0
            )
            moved = dot(swap, rows).astype(BF)
            for h in range(G):
                out_ref[y * G + h, t * G : (t + 1) * G, 0:W] = moved[h * E * C : (h + 1) * E * C, :]
                out_ref[y * G + h, t * G : (t + 1) * G, W:WP] = jnp.zeros((E * C, WP - W), BF)


def last(expert, recv, weight, act):
    vmem = pl.BlockSpec(memory_space=pltpu.VMEM)
    smem = pl.BlockSpec(memory_space=pltpu.SMEM)
    return pl.pallas_call(
        last_kernel,
        out_shape=(
            jax.ShapeDtypeStruct((Y * G, 2 * G, WP), BF),
            jax.ShapeDtypeStruct((Z, 3, W, S), BF),
        ),
        in_specs=[smem, vmem, vmem, vmem],
        out_specs=(vmem, vmem),
        scratch_shapes=[pltpu.VMEM((2, E, R, W), BF), pltpu.VMEM((2, E, R, W), F32)],
        name="last",
    )(expert, recv, weight, act)


def unpack_kernel(recv_ref, layer_ref, grad_ref):
    lane = lax.broadcasted_iota(jnp.int32, (G, WP), 1)
    for t, ref in enumerate((layer_ref, grad_ref)):
        for d in range(0, G, 2):
            rows = slice(t * G, (t + 1) * G)
            left = recv_ref[d, rows, :].astype(F32) + recv_ref[G + d, rows, :].astype(F32)
            right = recv_ref[d + 1, rows, :].astype(F32) + recv_ref[G + d + 1, rows, :].astype(F32)
            right = pltpu.roll(right, W - 256, 1)
            low = lane[:, 0:128] < W - 256
            at = d * W
            ref[:, at : at + 256] = left[:, 0:256].astype(BF)
            ref[:, at + 256 : at + 384] = jnp.where(low, left[:, 256:384], right[:, 0:128]).astype(BF)
            ref[:, at + 384 : at + 640] = right[:, 128:384].astype(BF)


def unpack(recv):
    vmem = pl.BlockSpec(memory_space=pltpu.VMEM)
    shape = jax.ShapeDtypeStruct((E * C, D), BF)
    return pl.pallas_call(
        unpack_kernel,
        out_shape=(shape, shape),
        in_specs=[vmem],
        out_specs=(vmem, vmem),
        name="unpack",
    )(recv)


def exchange(x, axes):
    return lax.all_to_all(x, axes, split_axis=0, concat_axis=0, tiled=True)


def body(tokens, cotangent, counts, destination, placement, gate_up_weight, down_weight):
    me = lax.axis_index(GRP).reshape(1).astype(jnp.int32)
    local = jnp.concatenate([gate_up_weight[0], down_weight], axis=0)
    weight = lax.all_gather(local[None], "z", axis=0, tiled=True)
    sent = pack(me, counts[0, 0], destination[0], tokens[0], cotangent[0])
    recv = exchange(sent, PLANE)
    near = lax.dynamic_index_in_dim(placement.reshape(Z, Y), lax.axis_index("y_hi"), 1, keepdims=False)
    expert = near // (Z * Y // E)
    parts = exchange(first(expert, recv, weight), GRP)
    act = lax.all_gather(middle(parts)[None], GRP, axis=0, tiled=True)
    returned, grads = last(expert, recv, weight, act)
    layer_out, input_grad = unpack(exchange(returned, PLANE))
    own = lax.psum_scatter(grads, "z", scatter_dimension=0, tiled=True).astype(F32)
    return (layer_out[None], input_grad[None], own[:, 0:2], own[:, 2])


def solution(mesh):
    fine = Mesh(mesh.devices.reshape(SIZES), AXES)
    return jax.shard_map(
        body,
        mesh=fine,
        in_specs=(
            P(GRP, EP, None),
            P(GRP, EP, None),
            P(GRP, EP, None),
            P(GRP, EP, None),
            P(),
            P(EP, None, GRP, None),
            P(EP, GRP, None),
        ),
        out_specs=(
            P(GRP, EP, None),
            P(GRP, EP, None),
            P(EP, None, GRP, None),
            P(EP, GRP, None),
        ),
        check_vma=False,
    )
```

```python
import jax
import jax.numpy as jnp
from jax import lax
from jax.experimental import pallas as pl
from jax.experimental.pallas import tpu as pltpu
from jax.sharding import Mesh, PartitionSpec as P

AXES = ("y_lo", "x", "core", "z_hi", "z_lo", "y_hi")
SIZES = (2, 4, 2, 8, 2, 2)
GRP = ("y_lo", "x", "core")
EP = ("z_hi", "z_lo", "y_hi")
NEAR = ("z_lo", "y_hi")
PLANE = NEAR + GRP

G = 16
Z = 8
N = 4
E = 4
C = 4
D = 5120
W = D // G
WP = 384
S = 128
Q = C * G
R = N * Q
H = Z * R // G
BF = jnp.bfloat16
F32 = jnp.float32
VMEM = pl.BlockSpec(memory_space=pltpu.VMEM)
SMEM = pl.BlockSpec(memory_space=pltpu.SMEM)
ANY = pl.BlockSpec(memory_space=pl.ANY)


def dot(a, b, dims=((1,), (0,))):
    return lax.dot_general(a, b, (dims, ((), ())), preferred_element_type=F32)


def pack_kernel(me_ref, counts_ref, dest_ref, tok_ref, cot_ref, out_ref):
    me = me_ref[0]
    rows = lax.broadcasted_iota(jnp.int32, (G, G), 0)
    pick = (rows == dest_ref[...]).astype(F32).astype(BF)
    lane = lax.broadcasted_iota(jnp.int32, (G, WP), 1)
    row = lax.broadcasted_iota(jnp.int32, (G, WP), 0)
    extra = jnp.zeros((G, WP), F32)
    for e in range(E):
        extra = jnp.where((lane == W + e) & (row == me), counts_ref[e].astype(F32), extra)
    for d in range(G):
        start = d * W // 128 * 128
        for t, ref in enumerate((tok_ref, cot_ref)):
            moved = dot(pick, ref[:, start : start + WP])
            if start != d * W:
                moved = pltpu.roll(moved, WP - (d * W - start), 1)
            moved = jnp.where(lane < W, moved, extra).astype(BF)
            for n in range(N):
                out_ref[n * G + d, t * G : (t + 1) * G, :] = moved


def pack(me, counts, dest, tokens, cotangent):
    return pl.pallas_call(
        pack_kernel,
        out_shape=jax.ShapeDtypeStruct((N * G, 2 * G, WP), BF),
        in_specs=[SMEM, SMEM, VMEM, VMEM, VMEM],
        out_specs=VMEM,
        name="pack",
    )(me, counts, dest, tokens, cotangent)


def rows_kernel(recv_ref, x_ref, xt_ref):
    lane = lax.broadcasted_iota(jnp.int32, (G, 128), 1)
    for n in range(N):
        table = jnp.zeros((G, 128), F32)
        for g in range(G):
            table = table + recv_ref[n * G + g, 0:G, WP - 128 : WP].astype(F32)
        for e in range(E):
            kept = jnp.sum(jnp.where(lane == 128 - (WP - W) + e, table, 0.0), axis=1, keepdims=True)
            kept = jnp.broadcast_to(kept, (G, W))
            for c in range(C):
                at = n * Q + c * G
                for t in range(2):
                    block = recv_ref[n * G + e * C + c, t * G : (t + 1) * G, 0:W].astype(F32)
                    x_ref[t, e, at : at + G, :] = jnp.where(kept > c + 0.5, block, 0.0).astype(BF)
    for t in range(2):
        for e in range(E):
            xt_ref[t, e] = x_ref[t, e].astype(F32).T.astype(BF)


def prepare(recv):
    return pl.pallas_call(
        rows_kernel,
        out_shape=(jax.ShapeDtypeStruct((2, E, R, W), BF), jax.ShapeDtypeStruct((2, E, W, R), BF)),
        in_specs=[VMEM],
        out_specs=(VMEM, VMEM),
        name="prepare",
    )(recv)


def first_kernel(expert_ref, x_ref, weight_ref, out_ref):
    for i in range(2):
        e = expert_ref[2 * pl.program_id(0) + i]
        tok = x_ref[0, e]
        out_ref[i, :, 0 : 2 * S] = dot(tok, jnp.concatenate([weight_ref[i, 0], weight_ref[i, 1]], axis=1)).astype(BF)
        out_ref[i, :, 2 * S : 3 * S] = dot(x_ref[1, e], weight_ref[i, 2]).astype(BF)


def first(expert, x, weight):
    return pl.pallas_call(
        first_kernel,
        grid=(Z // 2,),
        out_shape=jax.ShapeDtypeStruct((Z, R, 3 * S), BF),
        in_specs=[
            SMEM,
            pl.BlockSpec((2, E, R, W), lambda i: (0, 0, 0, 0)),
            pl.BlockSpec((2, 3, W, S), lambda i: (i, 0, 0, 0)),
        ],
        out_specs=pl.BlockSpec((2, R, 3 * S), lambda i: (i, 0, 0)),
        name="first",
    )(expert, x, weight)


def middle_kernel(part_ref, out_ref):
    total = part_ref[0].astype(F32)
    for d in range(1, G):
        total = total + part_ref[d].astype(F32)
    gate = total[:, 0:S]
    up = total[:, S : 2 * S]
    hidden_grad = total[:, 2 * S : 3 * S]
    sigmoid = jax.nn.sigmoid(gate)
    activated = gate * sigmoid
    hidden = (activated * up).astype(BF)
    gate_grad = (hidden_grad * up * sigmoid * (1.0 + gate * (1.0 - sigmoid))).astype(BF)
    up_grad = (hidden_grad * activated).astype(BF)
    for d in range(G):
        out_ref[d, :, 0:S] = hidden
        out_ref[d, :, S : 2 * S] = gate_grad
        out_ref[d, :, 2 * S : 3 * S] = up_grad


def middle(parts):
    block = pl.BlockSpec((G, H // 4, 3 * S), lambda i: (0, i, 0))
    return pl.pallas_call(
        middle_kernel,
        grid=(4,),
        out_shape=jax.ShapeDtypeStruct((G, H, 3 * S), BF),
        in_specs=[block],
        out_specs=block,
        name="middle",
    )(parts)


def weigh_kernel(expert_ref, xt_ref, act_ref, grad_ref, mark_ref):
    for i in range(2):
        e = expert_ref[2 * pl.program_id(0) + i]
        both = dot(xt_ref[0, e], act_ref[i, :, S : 3 * S])
        grad_ref[i, 0] = both[:, 0:S].astype(BF)
        grad_ref[i, 1] = both[:, S : 2 * S].astype(BF)
        grad_ref[i, 2] = dot(xt_ref[1, e], act_ref[i, :, 0:S]).astype(BF)
    mark_ref[...] = jnp.zeros_like(mark_ref)


def weigh(expert, xt, act):
    return pl.pallas_call(
        weigh_kernel,
        grid=(Z // 2,),
        out_shape=(jax.ShapeDtypeStruct((Z, 3, W, S), BF), jax.ShapeDtypeStruct((8, 128), F32)),
        in_specs=[
            SMEM,
            pl.BlockSpec((2, E, W, R), lambda i: (0, 0, 0, 0)),
            pl.BlockSpec((2, R, 3 * S), lambda i: (i, 0, 0)),
        ],
        out_specs=(pl.BlockSpec((2, 3, W, S), lambda i: (i, 0, 0, 0)), pl.BlockSpec((8, 128), lambda i: (0, 0))),
        name="weigh",
    )(expert, xt, act)


def last_kernel(expert_ref, weight_ref, act_ref, mark_ref, out_ref, acc_ref):
    acc_ref[...] = jnp.zeros_like(acc_ref)
    tail = ((1,), (1,))

    def step(z, carry):
        e = expert_ref[z]
        acc_ref[0, e] += dot(act_ref[z, :, 0:S], weight_ref[z, 2], tail)
        both = jnp.concatenate([weight_ref[z, 0], weight_ref[z, 1]], axis=1)
        acc_ref[1, e] += dot(act_ref[z, :, S : 3 * S], both, tail)
        return carry

    lax.fori_loop(0, Z, step, 0)
    size = E * Q
    i = lax.broadcasted_iota(jnp.int32, (size, size), 0)
    j = lax.broadcasted_iota(jnp.int32, (size, size), 1)
    swap = ((i // (E * C) == j % G) & (i % (E * C) == j // G)).astype(F32).astype(BF)
    for n in range(N):
        for t in range(2):
            rows = jnp.concatenate([acc_ref[t, e, n * Q : (n + 1) * Q, :].astype(BF) for e in range(E)], axis=0)
            moved = dot(swap, rows).astype(BF)
            for h in range(G):
                out_ref[n * G + h, t * G : (t + 1) * G, 0:W] = moved[h * E * C : (h + 1) * E * C, :]
                out_ref[n * G + h, t * G : (t + 1) * G, W:WP] = jnp.zeros((E * C, WP - W), BF)


def last(expert, weight, act, mark):
    return pl.pallas_call(
        last_kernel,
        out_shape=jax.ShapeDtypeStruct((N * G, 2 * G, WP), BF),
        in_specs=[SMEM, VMEM, VMEM, ANY],
        out_specs=VMEM,
        scratch_shapes=[pltpu.VMEM((2, E, R, W), F32)],
        name="last",
    )(expert, weight, act, mark)


def unpack_kernel(recv_ref, layer_ref, grad_ref):
    low = lax.broadcasted_iota(jnp.int32, (G, 128), 1) < W - 256
    for t, ref in enumerate((layer_ref, grad_ref)):
        rows = slice(t * G, (t + 1) * G)
        for d in range(0, G, 2):
            left = recv_ref[d, rows, :].astype(F32)
            right = recv_ref[d + 1, rows, :].astype(F32)
            for n in range(1, N):
                left = left + recv_ref[n * G + d, rows, :].astype(F32)
                right = right + recv_ref[n * G + d + 1, rows, :].astype(F32)
            right = pltpu.roll(right, W - 256, 1)
            at = d * W
            ref[:, at : at + 256] = left[:, 0:256].astype(BF)
            ref[:, at + 256 : at + 384] = jnp.where(low, left[:, 256:384], right[:, 0:128]).astype(BF)
            ref[:, at + 384 : at + 640] = right[:, 128:384].astype(BF)


def unpack(recv):
    shape = jax.ShapeDtypeStruct((E * C, D), BF)
    return pl.pallas_call(
        unpack_kernel, out_shape=(shape, shape), in_specs=[VMEM], out_specs=(VMEM, VMEM), name="unpack"
    )(recv)


def widen_kernel(own_ref, gate_up_ref, down_ref):
    gate_up_ref[0] = own_ref[0, 0:2].astype(F32)
    down_ref[0] = own_ref[0, 2].astype(F32)


def widen(own):
    return pl.pallas_call(
        widen_kernel,
        out_shape=(jax.ShapeDtypeStruct((1, 2, W, S), F32), jax.ShapeDtypeStruct((1, W, S), F32)),
        in_specs=[VMEM],
        out_specs=(VMEM, VMEM),
        name="widen",
    )(own)


def exchange(x, axes):
    return lax.all_to_all(x, axes, split_axis=0, concat_axis=0, tiled=True)


def body(tokens, cotangent, counts, destination, placement, gate_up_weight, down_weight):
    me = lax.axis_index(GRP).reshape(1).astype(jnp.int32)
    local = jnp.concatenate([gate_up_weight[0], down_weight], axis=0)
    weight = lax.all_gather(local[None], "z_hi", axis=0, tiled=True)
    x, xt = prepare(exchange(pack(me, counts[0, 0], destination[0], tokens[0], cotangent[0]), PLANE))
    near = lax.dynamic_index_in_dim(placement.reshape(Z, N), lax.axis_index(NEAR), 1, keepdims=False)
    expert = near // (Z * N // E)
    parts = exchange(first(expert, x, weight).reshape(G, H, 3 * S), GRP)
    act = exchange(middle(parts), GRP).reshape(Z, R, 3 * S)
    grads, mark = weigh(expert, xt, act)
    own = lax.psum_scatter(grads, "z_hi", scatter_dimension=0, tiled=True)
    layer_out, input_grad = unpack(exchange(last(expert, weight, act, mark), PLANE))
    gate_up_grad, down_grad = widen(own)
    return (layer_out[None], input_grad[None], gate_up_grad, down_grad)


def solution(mesh):
    fine = Mesh(mesh.devices.reshape(SIZES), AXES)
    return jax.shard_map(
        body,
        mesh=fine,
        in_specs=(
            P(GRP, EP, None),
            P(GRP, EP, None),
            P(GRP, EP, None),
            P(GRP, EP, None),
            P(),
            P(EP, None, GRP, None),
            P(EP, GRP, None),
        ),
        out_specs=(
            P(GRP, EP, None),
            P(GRP, EP, None),
            P(EP, None, GRP, None),
            P(EP, GRP, None),
        ),
        check_vma=False,
    )
```

```python
import jax
import jax.numpy as jnp
from jax import lax
from jax.experimental import pallas as pl
from jax.experimental.pallas import tpu as pltpu
from jax.sharding import Mesh, PartitionSpec as P


AXES = ("y_lo", "x", "core", "z_hi", "z_lo", "y_hi")
SIZES = (2, 4, 2, 8, 2, 2)
GRP = ("y_lo", "x", "core")
EP = ("z_hi", "z_lo", "y_hi")
NEAR = ("z_lo", "y_hi")
PLANE = NEAR + GRP

G = 16
Z = 8
N = 4
E = 4
C = 4
D = 5120
W = D // G
WP = 384
S = 128
Q = C * G
R = N * Q
H = Z * R // G
BF = jnp.bfloat16
F32 = jnp.float32
VMEM = pl.BlockSpec(memory_space=pltpu.VMEM)
SMEM = pl.BlockSpec(memory_space=pltpu.SMEM)


def dot(a, b, dims=((1,), (0,))):
    return lax.dot_general(a, b, (dims, ((), ())), preferred_element_type=F32)


def pack_kernel(me_ref, counts_ref, dest_ref, tok_ref, cot_ref, out_ref):
    me = me_ref[0]
    rows = lax.broadcasted_iota(jnp.int32, (G, G), 0)
    pick = (rows == dest_ref[...]).astype(F32).astype(BF)
    lane = lax.broadcasted_iota(jnp.int32, (G, WP), 1)
    row = lax.broadcasted_iota(jnp.int32, (G, WP), 0)
    extra = jnp.zeros((G, WP), F32)
    for e in range(E):
        extra = jnp.where((lane == W + e) & (row == me), counts_ref[e].astype(F32), extra)
    for d in range(G):
        start = d * W // 128 * 128
        for t, ref in enumerate((tok_ref, cot_ref)):
            moved = dot(pick, ref[:, start : start + WP])
            if start != d * W:
                moved = pltpu.roll(moved, WP - (d * W - start), 1)
            moved = jnp.where(lane < W, moved, extra).astype(BF)
            for n in range(N):
                out_ref[n * G + d, t * G : (t + 1) * G, :] = moved


def pack(me, counts, dest, tokens, cotangent):
    return pl.pallas_call(
        pack_kernel,
        out_shape=jax.ShapeDtypeStruct((N * G, 2 * G, WP), BF),
        in_specs=[SMEM, SMEM, VMEM, VMEM, VMEM],
        out_specs=VMEM,
        name="pack",
    )(me, counts, dest, tokens, cotangent)


def rows_kernel(recv_ref, x_ref, xt_ref):
    lane = lax.broadcasted_iota(jnp.int32, (G, 128), 1)
    for n in range(N):
        table = jnp.zeros((G, 128), F32)
        for g in range(G):
            table = table + recv_ref[n * G + g, 0:G, WP - 128 : WP].astype(F32)
        for e in range(E):
            kept = jnp.sum(jnp.where(lane == 128 - (WP - W) + e, table, 0.0), axis=1, keepdims=True)
            kept = jnp.broadcast_to(kept, (G, W))
            for c in range(C):
                at = n * Q + c * G
                for t in range(2):
                    block = recv_ref[n * G + e * C + c, t * G : (t + 1) * G, 0:W].astype(F32)
                    x_ref[t, e, at : at + G, :] = jnp.where(kept > c + 0.5, block, 0.0).astype(BF)
    for t in range(2):
        for e in range(E):
            xt_ref[t, e] = x_ref[t, e].astype(F32).T.astype(BF)


def prepare(recv):
    return pl.pallas_call(
        rows_kernel,
        out_shape=(jax.ShapeDtypeStruct((2, E, R, W), BF), jax.ShapeDtypeStruct((2, E, W, R), BF)),
        in_specs=[VMEM],
        out_specs=(VMEM, VMEM),
        name="prepare",
    )(recv)


def first_kernel(expert_ref, x_ref, gate_up_ref, down_ref, out_ref):
    for i in range(2):
        e = expert_ref[2 * pl.program_id(0) + i]
        both = jnp.concatenate([gate_up_ref[i, 0], gate_up_ref[i, 1]], axis=1)
        out_ref[i, :, 0 : 2 * S] = dot(x_ref[0, e], both).astype(BF)
        out_ref[i, :, 2 * S : 3 * S] = dot(x_ref[1, e], down_ref[i]).astype(BF)


def first(expert, x, gate_up, down):
    return pl.pallas_call(
        first_kernel,
        grid=(Z // 2,),
        out_shape=jax.ShapeDtypeStruct((Z, R, 3 * S), BF),
        in_specs=[
            SMEM,
            pl.BlockSpec((2, E, R, W), lambda i: (0, 0, 0, 0)),
            pl.BlockSpec((2, 2, W, S), lambda i: (i, 0, 0, 0)),
            pl.BlockSpec((2, W, S), lambda i: (i, 0, 0)),
        ],
        out_specs=pl.BlockSpec((2, R, 3 * S), lambda i: (i, 0, 0)),
        name="first",
    )(expert, x, gate_up, down)


def middle_kernel(part_ref, out_ref):
    total = part_ref[0].astype(F32)
    for d in range(1, G):
        total = total + part_ref[d].astype(F32)
    gate = total[:, 0:S]
    up = total[:, S : 2 * S]
    hidden_grad = total[:, 2 * S : 3 * S]
    sigmoid = jax.nn.sigmoid(gate)
    activated = gate * sigmoid
    hidden = (activated * up).astype(BF)
    gate_grad = (hidden_grad * up * sigmoid * (1.0 + gate * (1.0 - sigmoid))).astype(BF)
    up_grad = (hidden_grad * activated).astype(BF)
    for d in range(G):
        out_ref[d, :, 0:S] = hidden
        out_ref[d, :, S : 2 * S] = gate_grad
        out_ref[d, :, 2 * S : 3 * S] = up_grad


def middle(parts):
    block = pl.BlockSpec((G, H // 4, 3 * S), lambda i: (0, i, 0))
    return pl.pallas_call(
        middle_kernel,
        grid=(4,),
        out_shape=jax.ShapeDtypeStruct((G, H, 3 * S), BF),
        in_specs=[block],
        out_specs=block,
        name="middle",
    )(parts)


def weigh_kernel(expert_ref, xt_ref, act_ref, out_ref):
    for i in range(2):
        e = expert_ref[2 * pl.program_id(0) + i]
        both = dot(xt_ref[0, e], act_ref[i, :, S : 3 * S])
        out_ref[i, 0] = both[:, 0:S].astype(BF)
        out_ref[i, 1] = both[:, S : 2 * S].astype(BF)
        out_ref[i, 2] = dot(xt_ref[1, e], act_ref[i, :, 0:S]).astype(BF)


def weigh(expert, xt, act):
    return pl.pallas_call(
        weigh_kernel,
        grid=(Z // 2,),
        out_shape=jax.ShapeDtypeStruct((Z, 3, W, S), BF),
        in_specs=[
            SMEM,
            pl.BlockSpec((2, E, W, R), lambda i: (0, 0, 0, 0)),
            pl.BlockSpec((2, R, 3 * S), lambda i: (i, 0, 0)),
        ],
        out_specs=pl.BlockSpec((2, 3, W, S), lambda i: (i, 0, 0, 0)),
        name="weigh",
    )(expert, xt, act)


def last_kernel(expert_ref, gate_up_ref, down_ref, act_ref, out_ref, acc_ref):
    acc_ref[...] = jnp.zeros_like(acc_ref)
    tail = ((1,), (1,))

    def step(z, carry):
        e = expert_ref[z]
        acc_ref[0, e] += dot(act_ref[z, :, 0:S], down_ref[z], tail)
        both = jnp.concatenate([gate_up_ref[z, 0], gate_up_ref[z, 1]], axis=1)
        acc_ref[1, e] += dot(act_ref[z, :, S : 3 * S], both, tail)
        return carry

    lax.fori_loop(0, Z, step, 0)
    size = E * Q
    i = lax.broadcasted_iota(jnp.int32, (size, size), 0)
    j = lax.broadcasted_iota(jnp.int32, (size, size), 1)
    swap = ((i // (E * C) == j % G) & (i % (E * C) == j // G)).astype(F32).astype(BF)
    for n in range(N):
        for t in range(2):
            rows = jnp.concatenate([acc_ref[t, e, n * Q : (n + 1) * Q, :].astype(BF) for e in range(E)], axis=0)
            moved = dot(swap, rows).astype(BF)
            for h in range(G):
                out_ref[n * G + h, t * G : (t + 1) * G, 0:W] = moved[h * E * C : (h + 1) * E * C, :]
                out_ref[n * G + h, t * G : (t + 1) * G, W:WP] = jnp.zeros((E * C, WP - W), BF)


def last(expert, gate_up, down, act):
    return pl.pallas_call(
        last_kernel,
        out_shape=jax.ShapeDtypeStruct((N * G, 2 * G, WP), BF),
        in_specs=[SMEM, VMEM, VMEM, VMEM],
        out_specs=VMEM,
        scratch_shapes=[pltpu.VMEM((2, E, R, W), F32)],
        name="last",
    )(expert, gate_up, down, act)


def unpack_kernel(recv_ref, layer_ref, grad_ref):
    low = lax.broadcasted_iota(jnp.int32, (G, 128), 1) < W - 256
    for t, ref in enumerate((layer_ref, grad_ref)):
        rows = slice(t * G, (t + 1) * G)
        for d in range(0, G, 2):
            left = recv_ref[d, rows, :].astype(F32)
            right = recv_ref[d + 1, rows, :].astype(F32)
            for n in range(1, N):
                left = left + recv_ref[n * G + d, rows, :].astype(F32)
                right = right + recv_ref[n * G + d + 1, rows, :].astype(F32)
            right = pltpu.roll(right, W - 256, 1)
            at = d * W
            ref[:, at : at + 256] = left[:, 0:256].astype(BF)
            ref[:, at + 256 : at + 384] = jnp.where(low, left[:, 256:384], right[:, 0:128]).astype(BF)
            ref[:, at + 384 : at + 640] = right[:, 128:384].astype(BF)


def unpack(recv):
    shape = jax.ShapeDtypeStruct((E * C, D), BF)
    return pl.pallas_call(
        unpack_kernel, out_shape=(shape, shape), in_specs=[VMEM], out_specs=(VMEM, VMEM), name="unpack"
    )(recv)


def widen_kernel(own_ref, gate_up_ref, down_ref):
    gate_up_ref[0] = own_ref[0, 0:2].astype(F32)
    down_ref[0] = own_ref[0, 2].astype(F32)


def widen(own):
    return pl.pallas_call(
        widen_kernel,
        out_shape=(jax.ShapeDtypeStruct((1, 2, W, S), F32), jax.ShapeDtypeStruct((1, W, S), F32)),
        in_specs=[VMEM],
        out_specs=(VMEM, VMEM),
        name="widen",
    )(own)


def exchange(x, axes):
    return lax.all_to_all(x, axes, split_axis=0, concat_axis=0, tiled=True)


def gather(x):
    return lax.all_gather(x, "z_hi", axis=0, tiled=True)


def scatter(x):
    return lax.psum_scatter(x, "z_hi", scatter_dimension=0, tiled=True)


def body(tokens, cotangent, counts, destination, placement, gate_up_weight, down_weight):
    gate_up = gather(gate_up_weight)
    down = gather(down_weight)
    me = lax.axis_index(GRP).reshape(1).astype(jnp.int32)
    near = lax.dynamic_index_in_dim(placement.reshape(Z, N), lax.axis_index(NEAR), 1, keepdims=False)
    expert = near // (Z * N // E)
    sent = pack(me, counts[0, 0], destination[0], tokens[0], cotangent[0])
    x, xt = prepare(exchange(sent, PLANE))
    parts = first(expert, x, gate_up, down).reshape(G, H, 3 * S)
    act = middle(exchange(parts, GRP))
    act = exchange(act, GRP).reshape(Z, R, 3 * S)
    own = scatter(weigh(expert, xt, act))
    out = last(expert, gate_up, down, act)
    layer_out, input_grad = unpack(exchange(out, PLANE))
    gate_up_grad, down_grad = widen(own)
    return (layer_out[None], input_grad[None], gate_up_grad, down_grad)


def solution(mesh):
    fine = Mesh(mesh.devices.reshape(SIZES), AXES)
    return jax.shard_map(
        body,
        mesh=fine,
        in_specs=(
            P(GRP, EP, None),
            P(GRP, EP, None),
            P(GRP, EP, None),
            P(GRP, EP, None),
            P(),
            P(EP, None, GRP, None),
            P(EP, GRP, None),
        ),
        out_specs=(
            P(GRP, EP, None),
            P(GRP, EP, None),
            P(EP, None, GRP, None),
            P(EP, GRP, None),
        ),
        check_vma=False,
    )
```

```python
import jax
import jax.numpy as jnp
from jax import lax
from jax.experimental import pallas as pl
from jax.experimental.pallas import tpu as pltpu
from jax.sharding import Mesh, PartitionSpec as P


AXES = ("y_lo", "x", "core", "z_hi", "z_lo", "y_hi")
SIZES = (2, 4, 2, 8, 2, 2)
GRP = ("y_lo", "x", "core")
EP = ("z_hi", "z_lo", "y_hi")
NEAR = ("z_lo", "y_hi")
PLANE = ("y_hi",) + GRP

G = 16
Z = 8
Y = 2
N = 2 * Y
E = 4
C = 4
D = 5120
W = D // G
WP = 384
S = 128
Q = C * G
R = N * Q
H = Z * R // G
BF = jnp.bfloat16
F32 = jnp.float32
VMEM = pl.BlockSpec(memory_space=pltpu.VMEM)
SMEM = pl.BlockSpec(memory_space=pltpu.SMEM)


def dot(a, b, dims=((1,), (0,))):
    return lax.dot_general(a, b, (dims, ((), ())), preferred_element_type=F32)


def pack_kernel(me_ref, counts_ref, dest_ref, tok_ref, cot_ref, out_ref, one_ref):
    me = me_ref[0]
    rows = lax.broadcasted_iota(jnp.int32, (G, G), 0)
    pick = (rows == dest_ref[...]).astype(F32).astype(BF)
    lane = lax.broadcasted_iota(jnp.int32, (G, WP), 1)
    row = lax.broadcasted_iota(jnp.int32, (G, WP), 0)
    extra = jnp.zeros((G, WP), F32)
    for e in range(E):
        extra = jnp.where((lane == W + e) & (row == me), counts_ref[e].astype(F32), extra)
    for d in range(G):
        start = d * W // 128 * 128
        for t, ref in enumerate((tok_ref, cot_ref)):
            moved = dot(pick, ref[:, start : start + WP])
            if start != d * W:
                moved = pltpu.roll(moved, WP - (d * W - start), 1)
            moved = jnp.where(lane < W, moved, extra).astype(BF)
            one_ref[d, t * G : (t + 1) * G, :] = moved
            for y in range(Y):
                out_ref[y * G + d, t * G : (t + 1) * G, :] = moved


def pack(me, counts, dest, tokens, cotangent):
    return pl.pallas_call(
        pack_kernel,
        out_shape=(
            jax.ShapeDtypeStruct((Y * G, 2 * G, WP), BF),
            jax.ShapeDtypeStruct((G, 2 * G, WP), BF),
        ),
        in_specs=[SMEM, SMEM, VMEM, VMEM, VMEM],
        out_specs=(VMEM, VMEM),
        name="pack",
    )(me, counts, dest, tokens, cotangent)


def rows_kernel(own_ref, other_ref, x_ref, xt_ref):
    lane = lax.broadcasted_iota(jnp.int32, (G, 128), 1)
    for n in range(N):
        recv_ref = (own_ref, other_ref)[n // Y]
        first_block = n % Y * G
        table = jnp.zeros((G, 128), F32)
        for g in range(G):
            table = table + recv_ref[first_block + g, 0:G, WP - 128 : WP].astype(F32)
        for e in range(E):
            kept = jnp.sum(jnp.where(lane == 128 - (WP - W) + e, table, 0.0), axis=1, keepdims=True)
            kept = jnp.broadcast_to(kept, (G, W))
            for c in range(C):
                at = n * Q + c * G
                for t in range(2):
                    block = recv_ref[first_block + e * C + c, t * G : (t + 1) * G, 0:W].astype(F32)
                    x_ref[t, e, at : at + G, :] = jnp.where(kept > c + 0.5, block, 0.0).astype(BF)
    for t in range(2):
        for e in range(E):
            xt_ref[t, e] = x_ref[t, e].astype(F32).T.astype(BF)


def prepare(own, other):
    return pl.pallas_call(
        rows_kernel,
        out_shape=(jax.ShapeDtypeStruct((2, E, R, W), BF), jax.ShapeDtypeStruct((2, E, W, R), BF)),
        in_specs=[VMEM, VMEM],
        out_specs=(VMEM, VMEM),
        name="prepare",
    )(own, other)


def first_kernel(expert_ref, x_ref, weight_ref, out_ref):
    for i in range(2):
        e = expert_ref[2 * pl.program_id(0) + i]
        both = jnp.concatenate([weight_ref[i, 0], weight_ref[i, 1]], axis=1)
        out_ref[i, :, 0 : 2 * S] = dot(x_ref[0, e], both).astype(BF)
        out_ref[i, :, 2 * S : 3 * S] = dot(x_ref[1, e], weight_ref[i, 2]).astype(BF)


def first(expert, x, weight):
    return pl.pallas_call(
        first_kernel,
        grid=(Z // 2,),
        out_shape=jax.ShapeDtypeStruct((Z, R, 3 * S), BF),
        in_specs=[
            SMEM,
            pl.BlockSpec((2, E, R, W), lambda i: (0, 0, 0, 0)),
            pl.BlockSpec((2, 3, W, S), lambda i: (i, 0, 0, 0)),
        ],
        out_specs=pl.BlockSpec((2, R, 3 * S), lambda i: (i, 0, 0)),
        name="first",
    )(expert, x, weight)


def middle_kernel(part_ref, out_ref):
    total = part_ref[0].astype(F32)
    for d in range(1, G):
        total = total + part_ref[d].astype(F32)
    gate = total[:, 0:S]
    up = total[:, S : 2 * S]
    hidden_grad = total[:, 2 * S : 3 * S]
    sigmoid = jax.nn.sigmoid(gate)
    activated = gate * sigmoid
    hidden = (activated * up).astype(BF)
    gate_grad = (hidden_grad * up * sigmoid * (1.0 + gate * (1.0 - sigmoid))).astype(BF)
    up_grad = (hidden_grad * activated).astype(BF)
    for d in range(G):
        out_ref[d, :, 0:S] = hidden
        out_ref[d, :, S : 2 * S] = gate_grad
        out_ref[d, :, 2 * S : 3 * S] = up_grad


def middle(parts):
    block = pl.BlockSpec((G, H // 4, 3 * S), lambda i: (0, i, 0))
    return pl.pallas_call(
        middle_kernel,
        grid=(4,),
        out_shape=jax.ShapeDtypeStruct((G, H, 3 * S), BF),
        in_specs=[block],
        out_specs=block,
        name="middle",
    )(parts)


def weigh_kernel(expert_ref, xt_ref, act_ref, out_ref):
    for i in range(2):
        e = expert_ref[2 * pl.program_id(0) + i]
        both = dot(xt_ref[0, e], act_ref[i, :, S : 3 * S])
        out_ref[i, 0] = both[:, 0:S].astype(BF)
        out_ref[i, 1] = both[:, S : 2 * S].astype(BF)
        out_ref[i, 2] = dot(xt_ref[1, e], act_ref[i, :, 0:S]).astype(BF)


def weigh(expert, xt, act):
    return pl.pallas_call(
        weigh_kernel,
        grid=(Z // 2,),
        out_shape=jax.ShapeDtypeStruct((Z, 3, W, S), BF),
        in_specs=[
            SMEM,
            pl.BlockSpec((2, E, W, R), lambda i: (0, 0, 0, 0)),
            pl.BlockSpec((2, R, 3 * S), lambda i: (i, 0, 0)),
        ],
        out_specs=pl.BlockSpec((2, 3, W, S), lambda i: (i, 0, 0, 0)),
        name="weigh",
    )(expert, xt, act)


def last_kernel(expert_ref, weight_ref, act_ref, own_ref, other_ref, acc_ref):
    acc_ref[...] = jnp.zeros_like(acc_ref)
    tail = ((1,), (1,))

    def step(z, carry):
        e = expert_ref[z]
        acc_ref[0, e] += dot(act_ref[z, :, 0:S], weight_ref[z, 2], tail)
        both = jnp.concatenate([weight_ref[z, 0], weight_ref[z, 1]], axis=1)
        acc_ref[1, e] += dot(act_ref[z, :, S : 3 * S], both, tail)
        return carry

    lax.fori_loop(0, Z, step, 0)
    size = E * Q
    i = lax.broadcasted_iota(jnp.int32, (size, size), 0)
    j = lax.broadcasted_iota(jnp.int32, (size, size), 1)
    swap = ((i // (E * C) == j % G) & (i % (E * C) == j // G)).astype(F32).astype(BF)
    for n in range(N):
        out_ref = (own_ref, other_ref)[n // Y]
        first_block = n % Y * G
        for t in range(2):
            rows = jnp.concatenate([acc_ref[t, e, n * Q : (n + 1) * Q, :].astype(BF) for e in range(E)], axis=0)
            moved = dot(swap, rows).astype(BF)
            for h in range(G):
                out_ref[first_block + h, t * G : (t + 1) * G, 0:W] = moved[h * E * C : (h + 1) * E * C, :]
                out_ref[first_block + h, t * G : (t + 1) * G, W:WP] = jnp.zeros((E * C, WP - W), BF)


def last(expert, weight, act):
    shape = jax.ShapeDtypeStruct((Y * G, 2 * G, WP), BF)
    return pl.pallas_call(
        last_kernel,
        out_shape=(shape, shape),
        in_specs=[SMEM, VMEM, VMEM],
        out_specs=(VMEM, VMEM),
        scratch_shapes=[pltpu.VMEM((2, E, R, W), F32)],
        name="last",
    )(expert, weight, act)


def unpack_kernel(*refs):
    recv_ref, layer_ref, grad_ref = refs[0], refs[-2], refs[-1]
    add_refs = refs[1:-2]
    low = lax.broadcasted_iota(jnp.int32, (G, 128), 1) < W - 256
    for t, ref in enumerate((layer_ref, grad_ref)):
        rows = slice(t * G, (t + 1) * G)
        for d in range(0, G, 2):
            left = recv_ref[d, rows, :].astype(F32) + recv_ref[G + d, rows, :].astype(F32)
            right = recv_ref[d + 1, rows, :].astype(F32) + recv_ref[G + d + 1, rows, :].astype(F32)
            right = pltpu.roll(right, W - 256, 1)
            at = d * W
            cut = jnp.where(low, left[:, 256:384], right[:, 0:128])
            for lo, hi, part in ((0, 256, left[:, 0:256]), (256, 384, cut), (384, 640, right[:, 128:384])):
                if add_refs:
                    part = part + add_refs[t][:, at + lo : at + hi].astype(F32)
                ref[:, at + lo : at + hi] = part.astype(BF)


def unpack(recv, *add):
    shape = jax.ShapeDtypeStruct((E * C, D), BF)
    return pl.pallas_call(
        unpack_kernel,
        out_shape=(shape, shape),
        in_specs=[VMEM] * (1 + len(add)),
        out_specs=(VMEM, VMEM),
        name="unpack",
    )(recv, *add)


def widen_kernel(own_ref, gate_up_ref, down_ref):
    gate_up_ref[0] = own_ref[0, 0:2].astype(F32)
    down_ref[0] = own_ref[0, 2].astype(F32)


def widen(own):
    return pl.pallas_call(
        widen_kernel,
        out_shape=(jax.ShapeDtypeStruct((1, 2, W, S), F32), jax.ShapeDtypeStruct((1, W, S), F32)),
        in_specs=[VMEM],
        out_specs=(VMEM, VMEM),
        name="widen",
    )(own)


def exchange(x, axes):
    return lax.all_to_all(x, axes, split_axis=0, concat_axis=0, tiled=True)


def gather(x):
    return lax.all_gather(x, "z_hi", axis=0, tiled=True)


def scatter(x):
    return lax.psum_scatter(x, "z_hi", scatter_dimension=0, tiled=True)


def swap(*xs):
    return [lax.ppermute(x, "z_lo", ((0, 1), (1, 0))) for x in xs]


def body(tokens, cotangent, counts, destination, placement, gate_up_weight, down_weight):
    local = jnp.concatenate([gate_up_weight, down_weight[:, None]], axis=1)
    weight = gather(local)
    me = lax.axis_index(GRP).reshape(1).astype(jnp.int32)
    near = lax.dynamic_index_in_dim(placement.reshape(Z, N), lax.axis_index(NEAR), 1, keepdims=False)
    expert = near // (Z * N // E)
    sent, one = pack(me, counts[0, 0], destination[0], tokens[0], cotangent[0])
    (other,) = swap(one)
    own = exchange(sent, PLANE)
    other = exchange(jnp.concatenate([other] * Y, axis=0), PLANE)
    x, xt = prepare(own, other)
    parts = first(expert, x, weight).reshape(G, H, 3 * S)
    act = middle(exchange(parts, GRP))
    act = exchange(act, GRP).reshape(Z, R, 3 * S)
    reduced = scatter(weigh(expert, xt, act))
    own, other = last(expert, weight, act)
    other = unpack(exchange(other, PLANE))
    other = swap(*other)
    layer_out, input_grad = unpack(exchange(own, PLANE), *other)
    gate_up_grad, down_grad = widen(reduced)
    return (layer_out[None], input_grad[None], gate_up_grad, down_grad)


def solution(mesh):
    fine = Mesh(mesh.devices.reshape(SIZES), AXES)
    return jax.shard_map(
        body,
        mesh=fine,
        in_specs=(
            P(GRP, EP, None),
            P(GRP, EP, None),
            P(GRP, EP, None),
            P(GRP, EP, None),
            P(),
            P(EP, None, GRP, None),
            P(EP, GRP, None),
        ),
        out_specs=(
            P(GRP, EP, None),
            P(GRP, EP, None),
            P(EP, None, GRP, None),
            P(EP, GRP, None),
        ),
        check_vma=False,
    )
```

```python
import jax
import jax.numpy as jnp
from jax import lax
from jax.experimental import pallas as pl
from jax.experimental.pallas import tpu as pltpu
from jax.sharding import Mesh, PartitionSpec as P


AXES = ("y_lo", "x", "core", "z_hi", "z_lo", "y_hi")
SIZES = (2, 4, 2, 8, 2, 2)
GRP = ("y_lo", "x", "core")
EP = ("z_hi", "z_lo", "y_hi")
NEAR = ("z_lo", "y_hi")
PLANE = ("y_hi",) + GRP

G = 16
Z = 8
Y = 2
N = 2 * Y
E = 4
C = 4
D = 5120
W = D // G
WP = 384
S = 128
Q = C * G
R = N * Q
CHIPS = ("y_lo", "x")
H = R // 2
BF = jnp.bfloat16
F32 = jnp.float32
LIMIT = 24 << 20
VMEM = pl.BlockSpec(memory_space=pltpu.VMEM)
SMEM = pl.BlockSpec(memory_space=pltpu.SMEM)


def dot(a, b, dims=((1,), (0,))):
    return lax.dot_general(a, b, (dims, ((), ())), preferred_element_type=F32)


def pack_kernel(me_ref, counts_ref, dest_ref, tok_ref, cot_ref, out_ref, one_ref):
    me = me_ref[0]
    rows = lax.broadcasted_iota(jnp.int32, (G, G), 0)
    pick = (rows == dest_ref[...]).astype(F32).astype(BF)
    lane = lax.broadcasted_iota(jnp.int32, (G, WP), 1)
    row = lax.broadcasted_iota(jnp.int32, (G, WP), 0)
    extra = jnp.zeros((G, WP), F32)
    for e in range(E):
        extra = jnp.where((lane == W + e) & (row == me), counts_ref[e].astype(F32), extra)
    for d in range(G):
        start = d * W // 128 * 128
        for t, ref in enumerate((tok_ref, cot_ref)):
            moved = dot(pick, ref[:, start : start + WP])
            if start != d * W:
                moved = pltpu.roll(moved, WP - (d * W - start), 1)
            moved = jnp.where(lane < W, moved, extra).astype(BF)
            one_ref[d, t * G : (t + 1) * G, :] = moved
            for y in range(Y):
                out_ref[y * G + d, t * G : (t + 1) * G, :] = moved


def pack(me, counts, dest, tokens, cotangent):
    return pl.pallas_call(
        pack_kernel,
        out_shape=(
            jax.ShapeDtypeStruct((Y * G, 2 * G, WP), BF),
            jax.ShapeDtypeStruct((G, 2 * G, WP), BF),
        ),
        in_specs=[SMEM, SMEM, VMEM, VMEM, VMEM],
        out_specs=(VMEM, VMEM),
        name="pack",
    )(me, counts, dest, tokens, cotangent)


def rows_kernel(own_ref, other_ref, x_ref, xt_ref):
    lane = lax.broadcasted_iota(jnp.int32, (G, 128), 1)
    for n in range(N):
        recv_ref = (own_ref, other_ref)[n // Y]
        first_block = n % Y * G
        table = jnp.zeros((G, 128), F32)
        for g in range(G):
            table = table + recv_ref[first_block + g, 0:G, WP - 128 : WP].astype(F32)
        for e in range(E):
            kept = jnp.sum(jnp.where(lane == 128 - (WP - W) + e, table, 0.0), axis=1, keepdims=True)
            kept = jnp.broadcast_to(kept, (G, W))
            for c in range(C):
                at = n * Q + c * G
                for t in range(2):
                    block = recv_ref[first_block + e * C + c, t * G : (t + 1) * G, 0:W].astype(F32)
                    x_ref[t, e, at : at + G, :] = jnp.where(kept > c + 0.5, block, 0.0).astype(BF)
    for t in range(2):
        for e in range(E):
            xt_ref[t, e] = x_ref[t, e].astype(F32).T.astype(BF)


def prepare(own, other):
    return pl.pallas_call(
        rows_kernel,
        out_shape=(jax.ShapeDtypeStruct((2, E, R, W), BF), jax.ShapeDtypeStruct((2, E, W, R), BF)),
        in_specs=[VMEM, VMEM],
        out_specs=(VMEM, VMEM),
        name="prepare",
    )(own, other)


def first_kernel(expert_ref, half_ref, x_ref, weight_ref, *refs):
    out_ref = refs[-1]
    for i in range(Z // 2):
        e = expert_ref[Z // 2 * pl.program_id(0) + i]
        both = jnp.concatenate([weight_ref[i, 0], weight_ref[i, 1]], axis=1)
        gate_up = dot(x_ref[0, e], both)
        hidden_grad = dot(x_ref[1, e], weight_ref[i, 2])
        if len(refs) > 1:
            gate_up = gate_up + refs[0][i, :, 0 : 2 * S].astype(F32)
            hidden_grad = hidden_grad + refs[0][i, :, 2 * S : 3 * S].astype(F32)
        out_ref[i, :, 0 : 2 * S] = gate_up.astype(BF)
        out_ref[i, :, 2 * S : 3 * S] = hidden_grad.astype(BF)


def first(expert, half, x, weight, *add):
    rows = pl.BlockSpec((Z // 2, H, 3 * S), lambda i, expert, half: (i, 0, 0))
    return pl.pallas_call(
        first_kernel,
        out_shape=jax.ShapeDtypeStruct((Z, H, 3 * S), BF),
        grid_spec=pltpu.PrefetchScalarGridSpec(
            num_scalar_prefetch=2,
            grid=(2,),
            in_specs=[
                pl.BlockSpec((2, E, H, W), lambda i, expert, half: (0, 0, half[0], 0)),
                pl.BlockSpec((Z // 2, 3, W, S), lambda i, expert, half: (i, 0, 0, 0)),
            ]
            + [rows] * len(add),
            out_specs=rows,
        ),
        compiler_params=pltpu.CompilerParams(vmem_limit_bytes=LIMIT),
        name="first",
    )(expert, half, x, weight, *add)


def middle_kernel(part_ref, out_ref):
    total = part_ref[0].astype(F32)
    for d in range(1, Z):
        total = total + part_ref[d].astype(F32)
    gate = total[:, 0:S]
    up = total[:, S : 2 * S]
    hidden_grad = total[:, 2 * S : 3 * S]
    sigmoid = jax.nn.sigmoid(gate)
    activated = gate * sigmoid
    hidden = (activated * up).astype(BF)
    gate_grad = (hidden_grad * up * sigmoid * (1.0 + gate * (1.0 - sigmoid))).astype(BF)
    up_grad = (hidden_grad * activated).astype(BF)
    for d in range(Z):
        out_ref[d, :, 0:S] = hidden
        out_ref[d, :, S : 2 * S] = gate_grad
        out_ref[d, :, 2 * S : 3 * S] = up_grad


def middle(parts):
    block = pl.BlockSpec((Z, H // 2, 3 * S), lambda i: (0, i, 0))
    return pl.pallas_call(
        middle_kernel,
        grid=(2,),
        out_shape=jax.ShapeDtypeStruct((Z, H, 3 * S), BF),
        in_specs=[block],
        out_specs=block,
        compiler_params=pltpu.CompilerParams(vmem_limit_bytes=LIMIT),
        name="middle",
    )(parts)


def in_order(core, mine, other):
    low = jnp.broadcast_to(core, mine.shape) == 0
    return jnp.concatenate([jnp.where(low, mine, other), jnp.where(low, other, mine)], axis=0)


def weigh_kernel(expert_ref, core_ref, xt_ref, mine_ref, other_ref, out_ref):
    for i in range(Z // 2):
        e = expert_ref[Z // 2 * pl.program_id(0) + i]
        act = in_order(core_ref[0], mine_ref[i], other_ref[i])
        both = dot(xt_ref[0, e], act[:, S : 3 * S])
        out_ref[i, 0] = both[:, 0:S].astype(BF)
        out_ref[i, 1] = both[:, S : 2 * S].astype(BF)
        out_ref[i, 2] = dot(xt_ref[1, e], act[:, 0:S]).astype(BF)


def weigh(expert, core, xt, mine, other):
    rows = pl.BlockSpec((Z // 2, H, 3 * S), lambda i: (i, 0, 0))
    return pl.pallas_call(
        weigh_kernel,
        grid=(2,),
        out_shape=jax.ShapeDtypeStruct((Z, 3, W, S), BF),
        in_specs=[SMEM, SMEM, pl.BlockSpec((2, E, W, R), lambda i: (0, 0, 0, 0)), rows, rows],
        out_specs=pl.BlockSpec((Z // 2, 3, W, S), lambda i: (i, 0, 0, 0)),
        compiler_params=pltpu.CompilerParams(vmem_limit_bytes=LIMIT),
        name="weigh",
    )(expert, core, xt, mine, other)


def last_kernel(expert_ref, core_ref, weight_ref, mine_ref, far_ref, own_ref, other_ref, acc_ref):
    acc_ref[...] = jnp.zeros_like(acc_ref)
    tail = ((1,), (1,))

    def step(z, carry):
        e = expert_ref[z]
        act = in_order(core_ref[0], mine_ref[z], far_ref[z])
        acc_ref[0, e] += dot(act[:, 0:S], weight_ref[z, 2], tail)
        both = jnp.concatenate([weight_ref[z, 0], weight_ref[z, 1]], axis=1)
        acc_ref[1, e] += dot(act[:, S : 3 * S], both, tail)
        return carry

    lax.fori_loop(0, Z, step, 0)
    size = E * Q
    i = lax.broadcasted_iota(jnp.int32, (size, size), 0)
    j = lax.broadcasted_iota(jnp.int32, (size, size), 1)
    swap = ((i // (E * C) == j % G) & (i % (E * C) == j // G)).astype(F32).astype(BF)
    for n in range(N):
        out_ref = (own_ref, other_ref)[n // Y]
        first_block = n % Y * G
        for t in range(2):
            rows = jnp.concatenate([acc_ref[t, e, n * Q : (n + 1) * Q, :].astype(BF) for e in range(E)], axis=0)
            moved = dot(swap, rows).astype(BF)
            for h in range(G):
                out_ref[first_block + h, t * G : (t + 1) * G, 0:W] = moved[h * E * C : (h + 1) * E * C, :]
                out_ref[first_block + h, t * G : (t + 1) * G, W:WP] = jnp.zeros((E * C, WP - W), BF)


def last(expert, core, weight, mine, far):
    shape = jax.ShapeDtypeStruct((Y * G, 2 * G, WP), BF)
    return pl.pallas_call(
        last_kernel,
        out_shape=(shape, shape),
        in_specs=[SMEM, SMEM, VMEM, VMEM, VMEM],
        out_specs=(VMEM, VMEM),
        scratch_shapes=[pltpu.VMEM((2, E, R, W), F32)],
        name="last",
    )(expert, core, weight, mine, far)


def unpack_kernel(*refs):
    recv_ref, layer_ref, grad_ref = refs[0], refs[-2], refs[-1]
    add_refs = refs[1:-2]
    low = lax.broadcasted_iota(jnp.int32, (G, 128), 1) < W - 256
    for t, ref in enumerate((layer_ref, grad_ref)):
        rows = slice(t * G, (t + 1) * G)
        for d in range(0, G, 2):
            left = recv_ref[d, rows, :].astype(F32) + recv_ref[G + d, rows, :].astype(F32)
            right = recv_ref[d + 1, rows, :].astype(F32) + recv_ref[G + d + 1, rows, :].astype(F32)
            right = pltpu.roll(right, W - 256, 1)
            at = d * W
            cut = jnp.where(low, left[:, 256:384], right[:, 0:128])
            for lo, hi, part in ((0, 256, left[:, 0:256]), (256, 384, cut), (384, 640, right[:, 128:384])):
                if add_refs:
                    part = part + add_refs[t][:, at + lo : at + hi].astype(F32)
                ref[:, at + lo : at + hi] = part.astype(BF)


def unpack(recv, *add):
    shape = jax.ShapeDtypeStruct((E * C, D), BF)
    return pl.pallas_call(
        unpack_kernel,
        out_shape=(shape, shape),
        in_specs=[VMEM] * (1 + len(add)),
        out_specs=(VMEM, VMEM),
        name="unpack",
    )(recv, *add)


def widen_kernel(own_ref, gate_up_ref, down_ref):
    gate_up_ref[0] = own_ref[0, 0:2].astype(F32)
    down_ref[0] = own_ref[0, 2].astype(F32)


def widen(own):
    return pl.pallas_call(
        widen_kernel,
        out_shape=(jax.ShapeDtypeStruct((1, 2, W, S), F32), jax.ShapeDtypeStruct((1, W, S), F32)),
        in_specs=[VMEM],
        out_specs=(VMEM, VMEM),
        name="widen",
    )(own)


def exchange(x, axes):
    return lax.all_to_all(x, axes, split_axis=0, concat_axis=0, tiled=True)


def gather(x):
    return lax.all_gather(x, "z_hi", axis=0, tiled=True)


def scatter(x):
    return lax.psum_scatter(x, "z_hi", scatter_dimension=0, tiled=True)


def swap(*xs, axis="z_lo"):
    return [lax.ppermute(x, axis, ((0, 1), (1, 0))) for x in xs]


def swap_cores(x):
    return swap(x, axis="core")[0]


def body(tokens, cotangent, counts, destination, placement, gate_up_weight, down_weight):
    local = jnp.concatenate([gate_up_weight, down_weight[:, None]], axis=1)
    weight = gather(local)
    me = lax.axis_index(GRP).reshape(1).astype(jnp.int32)
    near = lax.dynamic_index_in_dim(placement.reshape(Z, N), lax.axis_index(NEAR), 1, keepdims=False)
    expert = near // (Z * N // E)
    sent, one = pack(me, counts[0, 0], destination[0], tokens[0], cotangent[0])
    (other,) = swap(one)
    own = exchange(sent, PLANE)
    other = exchange(jnp.concatenate([other] * Y, axis=0), PLANE)
    x, xt = prepare(own, other)
    core = lax.axis_index("core").reshape(1).astype(jnp.int32)
    got = swap_cores(first(expert, 1 - core, x, weight))
    parts = first(expert, core, x, weight, got)
    act = middle(exchange(parts, CHIPS))
    mine = exchange(act, CHIPS)
    far = swap_cores(mine)
    reduced = scatter(weigh(expert, core, xt, mine, far))
    own, other = last(expert, core, weight, mine, far)
    other = unpack(exchange(other, PLANE))
    other = swap(*other)
    layer_out, input_grad = unpack(exchange(own, PLANE), *other)
    gate_up_grad, down_grad = widen(reduced)
    return (layer_out[None], input_grad[None], gate_up_grad, down_grad)


def solution(mesh):
    fine = Mesh(mesh.devices.reshape(SIZES), AXES)
    return jax.shard_map(
        body,
        mesh=fine,
        in_specs=(
            P(GRP, EP, None),
            P(GRP, EP, None),
            P(GRP, EP, None),
            P(GRP, EP, None),
            P(),
            P(EP, None, GRP, None),
            P(EP, GRP, None),
        ),
        out_specs=(
            P(GRP, EP, None),
            P(GRP, EP, None),
            P(EP, None, GRP, None),
            P(EP, GRP, None),
        ),
        check_vma=False,
    )
```

```python
import jax
import jax.numpy as jnp
from jax import lax
from jax.experimental import pallas as pl
from jax.experimental.pallas import tpu as pltpu
from jax.sharding import Mesh, PartitionSpec as P


AXES = ("y_lo", "x", "core", "z_hi", "z_lo", "y_hi")
SIZES = (2, 4, 2, 8, 2, 2)
GRP = ("y_lo", "x", "core")
EP = ("z_hi", "z_lo", "y_hi")
NEAR = ("z_lo", "y_hi")
PLANE = ("y_hi",) + GRP

G = 16
Z = 8
Y = 2
N = 2 * Y
E = 4
C = 4
D = 5120
W = D // G
WP = 384
S = 128
Q = C * G
R = N * Q
CHIPS = ("y_lo", "x")
H = R // 2
BF = jnp.bfloat16
F32 = jnp.float32
LIMIT = 24 << 20
VMEM = pl.BlockSpec(memory_space=pltpu.VMEM)
SMEM = pl.BlockSpec(memory_space=pltpu.SMEM)


def dot(a, b, dims=((1,), (0,))):
    return lax.dot_general(a, b, (dims, ((), ())), preferred_element_type=F32)


def pack_kernel(me_ref, counts_ref, dest_ref, tok_ref, cot_ref, out_ref):
    me = me_ref[0]
    rows = lax.broadcasted_iota(jnp.int32, (G, G), 0)
    pick = (rows == dest_ref[...]).astype(F32).astype(BF)
    lane = lax.broadcasted_iota(jnp.int32, (G, WP), 1)
    row = lax.broadcasted_iota(jnp.int32, (G, WP), 0)
    extra = jnp.zeros((G, WP), F32)
    for e in range(E):
        extra = jnp.where((lane == W + e) & (row == me), counts_ref[e].astype(F32), extra)
    for d in range(G):
        start = d * W // 128 * 128
        for t, ref in enumerate((tok_ref, cot_ref)):
            moved = dot(pick, ref[:, start : start + WP])
            if start != d * W:
                moved = pltpu.roll(moved, WP - (d * W - start), 1)
            moved = jnp.where(lane < W, moved, extra).astype(BF)
            for y in range(Y):
                out_ref[y * G + d, t * G : (t + 1) * G, :] = moved


def pack(me, counts, dest, tokens, cotangent):
    return pl.pallas_call(
        pack_kernel,
        out_shape=jax.ShapeDtypeStruct((Y * G, 2 * G, WP), BF),
        in_specs=[SMEM, SMEM, VMEM, VMEM, VMEM],
        out_specs=VMEM,
        name="pack",
    )(me, counts, dest, tokens, cotangent)


def rows_kernel(own_ref, other_ref, x_ref, xt_ref):
    lane = lax.broadcasted_iota(jnp.int32, (G, 128), 1)
    for n in range(N):
        recv_ref = (own_ref, other_ref)[n // Y]
        first_block = n % Y * G
        table = jnp.zeros((G, 128), F32)
        for g in range(G):
            table = table + recv_ref[first_block + g, 0:G, WP - 128 : WP].astype(F32)
        for e in range(E):
            kept = jnp.sum(jnp.where(lane == 128 - (WP - W) + e, table, 0.0), axis=1, keepdims=True)
            kept = jnp.broadcast_to(kept, (G, W))
            for c in range(C):
                at = n * Q + c * G
                for t in range(2):
                    block = recv_ref[first_block + e * C + c, t * G : (t + 1) * G, 0:W].astype(F32)
                    x_ref[t, e, at : at + G, :] = jnp.where(kept > c + 0.5, block, 0.0).astype(BF)
    for t in range(2):
        for e in range(E):
            xt_ref[t, e] = x_ref[t, e].astype(F32).T.astype(BF)


def prepare(own, other):
    return pl.pallas_call(
        rows_kernel,
        out_shape=(jax.ShapeDtypeStruct((2, E, R, W), BF), jax.ShapeDtypeStruct((2, E, W, R), BF)),
        in_specs=[VMEM, VMEM],
        out_specs=(VMEM, VMEM),
        compiler_params=pltpu.CompilerParams(vmem_limit_bytes=LIMIT),
        name="prepare",
    )(own, other)


def first_kernel(expert_ref, half_ref, x_ref, weight_ref, *refs):
    out_ref = refs[-1]
    for i in range(Z // 2):
        e = expert_ref[Z // 2 * pl.program_id(0) + i]
        both = jnp.concatenate([weight_ref[i, 0], weight_ref[i, 1]], axis=1)
        gate_up = dot(x_ref[0, e], both)
        hidden_grad = dot(x_ref[1, e], weight_ref[i, 2])
        if len(refs) > 1:
            gate_up = gate_up + refs[0][i, :, 0 : 2 * S].astype(F32)
            hidden_grad = hidden_grad + refs[0][i, :, 2 * S : 3 * S].astype(F32)
        out_ref[i, :, 0 : 2 * S] = gate_up.astype(BF)
        out_ref[i, :, 2 * S : 3 * S] = hidden_grad.astype(BF)


def first(expert, half, x, weight, *add):
    rows = pl.BlockSpec((Z // 2, H, 3 * S), lambda i, expert, half: (i, 0, 0))
    return pl.pallas_call(
        first_kernel,
        out_shape=jax.ShapeDtypeStruct((Z, H, 3 * S), BF),
        grid_spec=pltpu.PrefetchScalarGridSpec(
            num_scalar_prefetch=2,
            grid=(2,),
            in_specs=[
                pl.BlockSpec((2, E, H, W), lambda i, expert, half: (0, 0, half[0], 0)),
                pl.BlockSpec((Z // 2, 3, W, S), lambda i, expert, half: (i, 0, 0, 0)),
            ]
            + [rows] * len(add),
            out_specs=rows,
        ),
        compiler_params=pltpu.CompilerParams(vmem_limit_bytes=LIMIT),
        name="first",
    )(expert, half, x, pltpu.with_memory_space_constraint(weight, pltpu.HBM), *add)


def middle_kernel(part_ref, out_ref):
    total = part_ref[0].astype(F32)
    for d in range(1, Z):
        total = total + part_ref[d].astype(F32)
    gate = total[:, 0:S]
    up = total[:, S : 2 * S]
    hidden_grad = total[:, 2 * S : 3 * S]
    sigmoid = jax.nn.sigmoid(gate)
    activated = gate * sigmoid
    hidden = (activated * up).astype(BF)
    gate_grad = (hidden_grad * up * sigmoid * (1.0 + gate * (1.0 - sigmoid))).astype(BF)
    up_grad = (hidden_grad * activated).astype(BF)
    for d in range(Z):
        out_ref[d, :, 0:S] = hidden
        out_ref[d, :, S : 2 * S] = gate_grad
        out_ref[d, :, 2 * S : 3 * S] = up_grad


def middle(parts):
    block = pl.BlockSpec((Z, H // 2, 3 * S), lambda i: (0, i, 0))
    return pl.pallas_call(
        middle_kernel,
        grid=(2,),
        out_shape=jax.ShapeDtypeStruct((Z, H, 3 * S), BF),
        in_specs=[block],
        out_specs=block,
        compiler_params=pltpu.CompilerParams(vmem_limit_bytes=LIMIT),
        name="middle",
    )(parts)


def in_order(core, mine, other):
    low = jnp.broadcast_to(core, mine.shape) == 0
    return jnp.concatenate([jnp.where(low, mine, other), jnp.where(low, other, mine)], axis=0)


def weigh_kernel(expert_ref, core_ref, xt_ref, mine_ref, other_ref, out_ref):
    for i in range(Z // 2):
        e = expert_ref[Z // 2 * pl.program_id(0) + i]
        act = in_order(core_ref[0], mine_ref[i], other_ref[i])
        both = dot(xt_ref[0, e], act[:, S : 3 * S])
        out_ref[i, 0] = both[:, 0:S].astype(BF)
        out_ref[i, 1] = both[:, S : 2 * S].astype(BF)
        out_ref[i, 2] = dot(xt_ref[1, e], act[:, 0:S]).astype(BF)


def weigh(expert, core, xt, mine, other):
    rows = pl.BlockSpec((Z // 2, H, 3 * S), lambda i: (i, 0, 0))
    return pl.pallas_call(
        weigh_kernel,
        grid=(2,),
        out_shape=jax.ShapeDtypeStruct((Z, 3, W, S), BF),
        in_specs=[SMEM, SMEM, pl.BlockSpec((2, E, W, R), lambda i: (0, 0, 0, 0)), rows, rows],
        out_specs=pl.BlockSpec((Z // 2, 3, W, S), lambda i: (i, 0, 0, 0)),
        compiler_params=pltpu.CompilerParams(vmem_limit_bytes=LIMIT),
        name="weigh",
    )(expert, core, xt, mine, other)


def last_kernel(expert_ref, core_ref, weight_ref, mine_ref, far_ref, own_ref, other_ref, acc_ref):
    acc_ref[...] = jnp.zeros_like(acc_ref)
    tail = ((1,), (1,))

    def step(z, carry):
        e = expert_ref[z]
        act = in_order(core_ref[0], mine_ref[z], far_ref[z])
        acc_ref[0, e] += dot(act[:, 0:S], weight_ref[z, 2], tail)
        both = jnp.concatenate([weight_ref[z, 0], weight_ref[z, 1]], axis=1)
        acc_ref[1, e] += dot(act[:, S : 3 * S], both, tail)
        return carry

    lax.fori_loop(0, Z, step, 0)
    size = E * Q
    i = lax.broadcasted_iota(jnp.int32, (size, size), 0)
    j = lax.broadcasted_iota(jnp.int32, (size, size), 1)
    swap = ((i // (E * C) == j % G) & (i % (E * C) == j // G)).astype(F32).astype(BF)
    for n in range(N):
        out_ref = (own_ref, other_ref)[n // Y]
        first_block = n % Y * G
        for t in range(2):
            rows = jnp.concatenate([acc_ref[t, e, n * Q : (n + 1) * Q, :].astype(BF) for e in range(E)], axis=0)
            moved = dot(swap, rows).astype(BF)
            for h in range(G):
                out_ref[first_block + h, t * G : (t + 1) * G, 0:W] = moved[h * E * C : (h + 1) * E * C, :]
                out_ref[first_block + h, t * G : (t + 1) * G, W:WP] = jnp.zeros((E * C, WP - W), BF)


def last(expert, core, weight, mine, far):
    shape = jax.ShapeDtypeStruct((Y * G, 2 * G, WP), BF)
    return pl.pallas_call(
        last_kernel,
        out_shape=(shape, shape),
        in_specs=[SMEM, SMEM, VMEM, VMEM, VMEM],
        out_specs=(VMEM, VMEM),
        scratch_shapes=[pltpu.VMEM((2, E, R, W), F32)],
        name="last",
    )(expert, core, weight, mine, far)


def unpack_rows(recv_ref, t):
    low = lax.broadcasted_iota(jnp.int32, (G, 128), 1) < W - 256
    rows = slice(t * G, (t + 1) * G)
    for d in range(0, G, 2):
        left = recv_ref[d, rows, :].astype(F32) + recv_ref[G + d, rows, :].astype(F32)
        right = recv_ref[d + 1, rows, :].astype(F32) + recv_ref[G + d + 1, rows, :].astype(F32)
        right = pltpu.roll(right, W - 256, 1)
        yield slice(d * W, d * W + 256), left[:, 0:256]
        yield slice(d * W + 256, d * W + 384), jnp.where(low, left[:, 256:384], right[:, 0:128])
        yield slice(d * W + 384, d * W + 640), right[:, 128:384]


def unpack_other_kernel(recv_ref, out_ref):
    for t in range(2):
        for at, part in unpack_rows(recv_ref, t):
            out_ref[t, :, at] = part.astype(BF)


def unpack_other(recv):
    return pl.pallas_call(
        unpack_other_kernel,
        out_shape=jax.ShapeDtypeStruct((2, E * C, D), BF),
        in_specs=[VMEM],
        out_specs=VMEM,
        compiler_params=pltpu.CompilerParams(vmem_limit_bytes=LIMIT),
        name="unpack_other",
    )(recv)


def unpack_own_kernel(recv_ref, add_ref, layer_ref, grad_ref):
    for t, ref in enumerate((layer_ref, grad_ref)):
        for at, part in unpack_rows(recv_ref, t):
            ref[:, at] = (part + add_ref[t, :, at].astype(F32)).astype(BF)


def unpack_own(recv, add):
    shape = jax.ShapeDtypeStruct((E * C, D), BF)
    return pl.pallas_call(
        unpack_own_kernel,
        out_shape=(shape, shape),
        in_specs=[VMEM, VMEM],
        out_specs=(VMEM, VMEM),
        compiler_params=pltpu.CompilerParams(vmem_limit_bytes=LIMIT),
        name="unpack_own",
    )(recv, add)


def widen_kernel(own_ref, gate_up_ref, down_ref):
    gate_up_ref[0] = own_ref[0, 0:2].astype(F32)
    down_ref[0] = own_ref[0, 2].astype(F32)


def widen(own):
    return pl.pallas_call(
        widen_kernel,
        out_shape=(jax.ShapeDtypeStruct((1, 2, W, S), F32), jax.ShapeDtypeStruct((1, W, S), F32)),
        in_specs=[VMEM],
        out_specs=(VMEM, VMEM),
        name="widen",
    )(own)


def exchange(x, axes):
    return lax.all_to_all(x, axes, split_axis=0, concat_axis=0, tiled=True)


def gather(x):
    return lax.all_gather(x, "z_hi", axis=0, tiled=True)


def scatter(x):
    return lax.psum_scatter(x, "z_hi", scatter_dimension=0, tiled=True)


def swap(*xs, axis="z_lo"):
    return [lax.ppermute(x, axis, ((0, 1), (1, 0))) for x in xs]


def swap_cores(x):
    return swap(x, axis="core")[0]


def body(tokens, cotangent, counts, destination, placement, gate_up_weight, down_weight):
    local = jnp.concatenate([gate_up_weight, down_weight[:, None]], axis=1)
    weight = gather(local)
    me = lax.axis_index(GRP).reshape(1).astype(jnp.int32)
    near = lax.dynamic_index_in_dim(placement.reshape(Z, N), lax.axis_index(NEAR), 1, keepdims=False)
    expert = near // (Z * N // E)
    rows = jnp.concatenate([tokens, cotangent], axis=0)
    table = jnp.concatenate([counts[0, 0], destination[0, 0]])[None]
    far_table, far_rows = swap(table, rows)
    sent = pack(me, counts[0, 0], destination[0], tokens[0], cotangent[0])
    own = exchange(sent, PLANE)
    sent = pack(me, far_table[0, 0:E], far_table[:, E:], far_rows[0], far_rows[1])
    other = exchange(sent, PLANE)
    x, xt = prepare(own, other)
    core = lax.axis_index("core").reshape(1).astype(jnp.int32)
    got = swap_cores(first(expert, 1 - core, x, weight))
    parts = first(expert, core, x, weight, got)
    act = middle(exchange(parts, CHIPS))
    mine = exchange(act, CHIPS)
    far = swap_cores(mine)
    reduced = scatter(weigh(expert, core, xt, mine, far))
    own, other = last(expert, core, weight, mine, far)
    other = unpack_other(exchange(other, PLANE))
    (other,) = swap(other)
    layer_out, input_grad = unpack_own(exchange(own, PLANE), other)
    gate_up_grad, down_grad = widen(reduced)
    return (layer_out[None], input_grad[None], gate_up_grad, down_grad)


def solution(mesh):
    fine = Mesh(mesh.devices.reshape(SIZES), AXES)
    return jax.shard_map(
        body,
        mesh=fine,
        in_specs=(
            P(GRP, EP, None),
            P(GRP, EP, None),
            P(GRP, EP, None),
            P(GRP, EP, None),
            P(),
            P(EP, None, GRP, None),
            P(EP, GRP, None),
        ),
        out_specs=(
            P(GRP, EP, None),
            P(GRP, EP, None),
            P(EP, None, GRP, None),
            P(EP, GRP, None),
        ),
        check_vma=False,
    )
```

```python
import jax
import jax.numpy as jnp
from jax import lax
from jax.experimental import pallas as pl
from jax.experimental.pallas import tpu as pltpu
from jax.sharding import Mesh, PartitionSpec as P


AXES = ("y_lo", "x", "core", "z_hi", "z_lo", "y_hi")
SIZES = (2, 4, 2, 8, 2, 2)
GRP = ("y_lo", "x", "core")
EP = ("z_hi", "z_lo", "y_hi")
NEAR = ("z_lo", "y_hi")
PLANE = ("y_hi",) + GRP

G = 16
Z = 8
Y = 2
N = 2 * Y
E = 4
C = 4
D = 5120
W = D // G
WP = 384
S = 128
Q = C * G
R = N * Q
CHIPS = ("y_lo", "x")
H = R // 2
BF = jnp.bfloat16
F32 = jnp.float32
LIMIT = 24 << 20
VMEM = pl.BlockSpec(memory_space=pltpu.VMEM)
SMEM = pl.BlockSpec(memory_space=pltpu.SMEM)


def dot(a, b, dims=((1,), (0,))):
    return lax.dot_general(a, b, (dims, ((), ())), preferred_element_type=F32)


def pack_kernel(me_ref, counts_ref, dest_ref, tok_ref, cot_ref, out_ref):
    me = me_ref[0]
    rows = lax.broadcasted_iota(jnp.int32, (G, G), 0)
    pick = (rows == dest_ref[...]).astype(F32).astype(BF)
    lane = lax.broadcasted_iota(jnp.int32, (G, WP), 1)
    row = lax.broadcasted_iota(jnp.int32, (G, WP), 0)
    extra = jnp.zeros((G, WP), F32)
    for e in range(E):
        extra = jnp.where((lane == W + e) & (row == me), counts_ref[e].astype(F32), extra)
    for d in range(G):
        start = d * W // 128 * 128
        for t, ref in enumerate((tok_ref, cot_ref)):
            moved = dot(pick, ref[:, start : start + WP])
            if start != d * W:
                moved = pltpu.roll(moved, WP - (d * W - start), 1)
            moved = jnp.where(lane < W, moved, extra).astype(BF)
            for y in range(Y):
                out_ref[y * G + d, t * G : (t + 1) * G, :] = moved


def pack(me, counts, dest, tokens, cotangent):
    return pl.pallas_call(
        pack_kernel,
        out_shape=jax.ShapeDtypeStruct((Y * G, 2 * G, WP), BF),
        in_specs=[SMEM, SMEM, VMEM, VMEM, VMEM],
        out_specs=VMEM,
        name="pack",
    )(me, counts, dest, tokens, cotangent)


def rows_kernel(own_ref, other_ref, x_ref, xt_ref):
    lane = lax.broadcasted_iota(jnp.int32, (G, 128), 1)
    for n in range(N):
        recv_ref = (own_ref, other_ref)[n // Y]
        first_block = n % Y * G
        table = jnp.zeros((G, 128), F32)
        for g in range(G):
            table = table + recv_ref[first_block + g, 0:G, WP - 128 : WP].astype(F32)
        for e in range(E):
            kept = jnp.sum(jnp.where(lane == 128 - (WP - W) + e, table, 0.0), axis=1, keepdims=True)
            kept = jnp.broadcast_to(kept, (G, W))
            for c in range(C):
                at = n * Q + c * G
                for t in range(2):
                    block = recv_ref[first_block + e * C + c, t * G : (t + 1) * G, 0:W].astype(F32)
                    x_ref[t, e, at : at + G, :] = jnp.where(kept > c + 0.5, block, 0.0).astype(BF)
    for t in range(2):
        for e in range(E):
            xt_ref[t, e] = x_ref[t, e].astype(F32).T.astype(BF)


def prepare(own, other):
    return pl.pallas_call(
        rows_kernel,
        out_shape=(jax.ShapeDtypeStruct((2, E, R, W), BF), jax.ShapeDtypeStruct((2, E, W, R), BF)),
        in_specs=[VMEM, VMEM],
        out_specs=(VMEM, VMEM),
        compiler_params=pltpu.CompilerParams(vmem_limit_bytes=LIMIT),
        name="prepare",
    )(own, other)


def first_kernel(expert_ref, half_ref, x_ref, weight_ref, out_ref):
    for i in range(Z // 2):
        e = expert_ref[Z // 2 * pl.program_id(0) + i]
        both = jnp.concatenate([weight_ref[i, 0], weight_ref[i, 1]], axis=1)
        out_ref[i, :, 0 : 2 * S] = dot(x_ref[0, e], both).astype(out_ref.dtype)
        out_ref[i, :, 2 * S : 3 * S] = dot(x_ref[1, e], weight_ref[i, 2]).astype(out_ref.dtype)


def first(expert, half, x, weight, dtype):
    return pl.pallas_call(
        first_kernel,
        out_shape=jax.ShapeDtypeStruct((Z, H, 3 * S), dtype),
        grid_spec=pltpu.PrefetchScalarGridSpec(
            num_scalar_prefetch=2,
            grid=(2,),
            in_specs=[
                pl.BlockSpec((2, E, H, W), lambda i, expert, half: (0, 0, half[0], 0)),
                pl.BlockSpec((Z // 2, 3, W, S), lambda i, expert, half: (i, 0, 0, 0)),
            ],
            out_specs=pl.BlockSpec((Z // 2, H, 3 * S), lambda i, expert, half: (i, 0, 0)),
        ),
        compiler_params=pltpu.CompilerParams(vmem_limit_bytes=LIMIT),
        name="first",
    )(expert, half, x, weight)


def add_kernel(keep_ref, got_ref, out_ref):
    for z in range(Z):
        out_ref[z] = (keep_ref[z] + got_ref[z].astype(F32)).astype(BF)


def add_cores(keep, got):
    return pl.pallas_call(
        add_kernel,
        out_shape=jax.ShapeDtypeStruct((Z, H, 3 * S), BF),
        in_specs=[VMEM, VMEM],
        out_specs=VMEM,
        compiler_params=pltpu.CompilerParams(vmem_limit_bytes=LIMIT),
        name="add_cores",
    )(keep, got)


def middle_kernel(part_ref, out_ref):
    total = part_ref[0].astype(F32)
    for d in range(1, Z):
        total = total + part_ref[d].astype(F32)
    gate = total[:, 0:S]
    up = total[:, S : 2 * S]
    hidden_grad = total[:, 2 * S : 3 * S]
    sigmoid = jax.nn.sigmoid(gate)
    activated = gate * sigmoid
    hidden = (activated * up).astype(BF)
    gate_grad = (hidden_grad * up * sigmoid * (1.0 + gate * (1.0 - sigmoid))).astype(BF)
    up_grad = (hidden_grad * activated).astype(BF)
    for d in range(Z):
        out_ref[d, :, 0:S] = hidden
        out_ref[d, :, S : 2 * S] = gate_grad
        out_ref[d, :, 2 * S : 3 * S] = up_grad


def middle(parts):
    block = pl.BlockSpec((Z, H // 2, 3 * S), lambda i: (0, i, 0))
    return pl.pallas_call(
        middle_kernel,
        grid=(2,),
        out_shape=jax.ShapeDtypeStruct((Z, H, 3 * S), BF),
        in_specs=[block],
        out_specs=block,
        compiler_params=pltpu.CompilerParams(vmem_limit_bytes=LIMIT),
        name="middle",
    )(parts)


def in_order(core, mine, other):
    low = jnp.broadcast_to(core, mine.shape) == 0
    return jnp.concatenate([jnp.where(low, mine, other), jnp.where(low, other, mine)], axis=0)


def weigh_kernel(expert_ref, core_ref, xt_ref, mine_ref, other_ref, out_ref):
    for i in range(Z // 2):
        e = expert_ref[Z // 2 * pl.program_id(0) + i]
        act = in_order(core_ref[0], mine_ref[i], other_ref[i])
        both = dot(xt_ref[0, e], act[:, S : 3 * S])
        out_ref[i, 0] = both[:, 0:S].astype(BF)
        out_ref[i, 1] = both[:, S : 2 * S].astype(BF)
        out_ref[i, 2] = dot(xt_ref[1, e], act[:, 0:S]).astype(BF)


def weigh(expert, core, xt, mine, other):
    rows = pl.BlockSpec((Z // 2, H, 3 * S), lambda i: (i, 0, 0))
    return pl.pallas_call(
        weigh_kernel,
        grid=(2,),
        out_shape=pltpu.HBM((Z, 3, W, S), BF),
        in_specs=[SMEM, SMEM, pl.BlockSpec((2, E, W, R), lambda i: (0, 0, 0, 0)), rows, rows],
        out_specs=pl.BlockSpec((Z // 2, 3, W, S), lambda i: (i, 0, 0, 0)),
        compiler_params=pltpu.CompilerParams(vmem_limit_bytes=LIMIT),
        name="weigh",
    )(expert, core, xt, mine, other)


def last_kernel(expert_ref, core_ref, weight_ref, mine_ref, far_ref, own_ref, other_ref, acc_ref):
    acc_ref[...] = jnp.zeros_like(acc_ref)
    tail = ((1,), (1,))

    def step(z, carry):
        e = expert_ref[z]
        act = in_order(core_ref[0], mine_ref[z], far_ref[z])
        acc_ref[0, e] += dot(act[:, 0:S], weight_ref[z, 2], tail)
        both = jnp.concatenate([weight_ref[z, 0], weight_ref[z, 1]], axis=1)
        acc_ref[1, e] += dot(act[:, S : 3 * S], both, tail)
        return carry

    lax.fori_loop(0, Z, step, 0)
    size = E * Q
    i = lax.broadcasted_iota(jnp.int32, (size, size), 0)
    j = lax.broadcasted_iota(jnp.int32, (size, size), 1)
    swap = ((i // (E * C) == j % G) & (i % (E * C) == j // G)).astype(F32).astype(BF)
    for n in range(N):
        out_ref = (own_ref, other_ref)[n // Y]
        first_block = n % Y * G
        for t in range(2):
            rows = jnp.concatenate([acc_ref[t, e, n * Q : (n + 1) * Q, :].astype(BF) for e in range(E)], axis=0)
            moved = dot(swap, rows).astype(BF)
            for h in range(G):
                out_ref[first_block + h, t * G : (t + 1) * G, 0:W] = moved[h * E * C : (h + 1) * E * C, :]
                out_ref[first_block + h, t * G : (t + 1) * G, W:WP] = jnp.zeros((E * C, WP - W), BF)


def last(expert, core, weight, mine, far):
    shape = jax.ShapeDtypeStruct((Y * G, 2 * G, WP), BF)
    return pl.pallas_call(
        last_kernel,
        out_shape=(shape, shape),
        in_specs=[SMEM, SMEM, VMEM, VMEM, VMEM],
        out_specs=(VMEM, VMEM),
        scratch_shapes=[pltpu.VMEM((2, E, R, W), F32)],
        compiler_params=pltpu.CompilerParams(vmem_limit_bytes=LIMIT),
        name="last",
    )(expert, core, weight, mine, far)


def unpack_rows(recv_ref, t):
    low = lax.broadcasted_iota(jnp.int32, (G, 128), 1) < W - 256
    rows = slice(t * G, (t + 1) * G)
    for d in range(0, G, 2):
        left = recv_ref[d, rows, :].astype(F32) + recv_ref[G + d, rows, :].astype(F32)
        right = recv_ref[d + 1, rows, :].astype(F32) + recv_ref[G + d + 1, rows, :].astype(F32)
        right = pltpu.roll(right, W - 256, 1)
        yield slice(d * W, d * W + 256), left[:, 0:256]
        yield slice(d * W + 256, d * W + 384), jnp.where(low, left[:, 256:384], right[:, 0:128])
        yield slice(d * W + 384, d * W + 640), right[:, 128:384]


def unpack_other_kernel(recv_ref, out_ref):
    for t in range(2):
        for at, part in unpack_rows(recv_ref, t):
            out_ref[t, :, at] = part.astype(BF)


def unpack_other(recv):
    return pl.pallas_call(
        unpack_other_kernel,
        out_shape=jax.ShapeDtypeStruct((2, E * C, D), BF),
        in_specs=[VMEM],
        out_specs=VMEM,
        compiler_params=pltpu.CompilerParams(vmem_limit_bytes=LIMIT),
        name="unpack_other",
    )(recv)


def unpack_own_kernel(recv_ref, add_ref, layer_ref, grad_ref):
    for t, ref in enumerate((layer_ref, grad_ref)):
        for at, part in unpack_rows(recv_ref, t):
            ref[:, at] = (part + add_ref[t, :, at].astype(F32)).astype(BF)


def unpack_own(recv, add):
    shape = jax.ShapeDtypeStruct((E * C, D), BF)
    return pl.pallas_call(
        unpack_own_kernel,
        out_shape=(shape, shape),
        in_specs=[VMEM, VMEM],
        out_specs=(VMEM, VMEM),
        compiler_params=pltpu.CompilerParams(vmem_limit_bytes=LIMIT),
        name="unpack_own",
    )(recv, add)


def widen_kernel(own_ref, gate_up_ref, down_ref):
    gate_up_ref[0] = own_ref[0, 0:2].astype(F32)
    down_ref[0] = own_ref[0, 2].astype(F32)


def widen(own):
    return pl.pallas_call(
        widen_kernel,
        out_shape=(jax.ShapeDtypeStruct((1, 2, W, S), F32), jax.ShapeDtypeStruct((1, W, S), F32)),
        in_specs=[VMEM],
        out_specs=(VMEM, VMEM),
        name="widen",
    )(own)


def exchange(x, axes):
    return lax.all_to_all(x, axes, split_axis=0, concat_axis=0, tiled=True)


def gather(x):
    return lax.all_gather(x, "z_hi", axis=0, tiled=True)


def scatter(x):
    return lax.psum_scatter(x, "z_hi", scatter_dimension=0, tiled=True)


def swap(*xs, axis="z_lo"):
    return [lax.ppermute(x, axis, ((0, 1), (1, 0))) for x in xs]


def swap_cores(x):
    return swap(x, axis="core")[0]


def body(tokens, cotangent, counts, destination, placement, gate_up_weight, down_weight):
    local = jnp.concatenate([gate_up_weight, down_weight[:, None]], axis=1)
    weight = gather(local)
    me = lax.axis_index(GRP).reshape(1).astype(jnp.int32)
    near = lax.dynamic_index_in_dim(placement.reshape(Z, N), lax.axis_index(NEAR), 1, keepdims=False)
    expert = near // (Z * N // E)
    rows = jnp.concatenate([tokens, cotangent], axis=0)
    table = jnp.concatenate([counts[0, 0], destination[0, 0]])[None]
    far_table, far_rows = swap(table, rows)
    sent = pack(me, counts[0, 0], destination[0], tokens[0], cotangent[0])
    own = exchange(sent, PLANE)
    sent = pack(me, far_table[0, 0:E], far_table[:, E:], far_rows[0], far_rows[1])
    other = exchange(sent, PLANE)
    x, xt = prepare(own, other)
    core = lax.axis_index("core").reshape(1).astype(jnp.int32)
    streamed = pltpu.with_memory_space_constraint(weight, pltpu.HBM)
    got = swap_cores(first(expert, 1 - core, x, streamed, BF))
    keep = first(expert, core, x, weight, F32)
    parts = add_cores(keep, got)
    act = middle(exchange(parts, CHIPS))
    mine = exchange(act, CHIPS)
    far = swap_cores(mine)
    reduced = scatter(weigh(expert, core, xt, mine, far))
    own, other = last(expert, core, weight, mine, far)
    other = unpack_other(exchange(other, PLANE))
    (other,) = swap(other)
    layer_out, input_grad = unpack_own(exchange(own, PLANE), other)
    gate_up_grad, down_grad = widen(reduced)
    return (layer_out[None], input_grad[None], gate_up_grad, down_grad)


def solution(mesh):
    fine = Mesh(mesh.devices.reshape(SIZES), AXES)
    return jax.shard_map(
        body,
        mesh=fine,
        in_specs=(
            P(GRP, EP, None),
            P(GRP, EP, None),
            P(GRP, EP, None),
            P(GRP, EP, None),
            P(),
            P(EP, None, GRP, None),
            P(EP, GRP, None),
        ),
        out_specs=(
            P(GRP, EP, None),
            P(GRP, EP, None),
            P(EP, None, GRP, None),
            P(EP, GRP, None),
        ),
        check_vma=False,
    )
```

```python
import jax
import jax.numpy as jnp
from jax import lax
from jax.experimental import pallas as pl
from jax.experimental.pallas import tpu as pltpu
from jax.sharding import Mesh, PartitionSpec as P


AXES = ("y_lo", "x", "core", "z_hi", "z_lo", "y_hi")
SIZES = (2, 4, 2, 8, 2, 2)
GRP = ("y_lo", "x", "core")
EP = ("z_hi", "z_lo", "y_hi")
NEAR = ("z_lo", "y_hi")
PLANE = ("y_hi",) + GRP

G = 16
Z = 8
Y = 2
N = 2 * Y
E = 4
C = 4
D = 5120
W = D // G
WP = 384
S = 128
Q = C * G
R = N * Q
CHIPS = ("y_lo", "x")
H = R // 2
BF = jnp.bfloat16
F32 = jnp.float32
LIMIT = 24 << 20
VMEM = pl.BlockSpec(memory_space=pltpu.VMEM)
SMEM = pl.BlockSpec(memory_space=pltpu.SMEM)


def dot(a, b, dims=((1,), (0,))):
    return lax.dot_general(a, b, (dims, ((), ())), preferred_element_type=F32)


def pack_kernel(me_ref, counts_ref, dest_ref, tok_ref, cot_ref, out_ref):
    me = me_ref[0]
    rows = lax.broadcasted_iota(jnp.int32, (G, G), 0)
    pick = (rows == dest_ref[...]).astype(F32).astype(BF)
    lane = lax.broadcasted_iota(jnp.int32, (G, WP), 1)
    row = lax.broadcasted_iota(jnp.int32, (G, WP), 0)
    extra = jnp.zeros((G, WP), F32)
    for e in range(E):
        extra = jnp.where((lane == W + e) & (row == me), counts_ref[e].astype(F32), extra)
    for d in range(G):
        start = d * W // 128 * 128
        for t, ref in enumerate((tok_ref, cot_ref)):
            moved = dot(pick, ref[:, start : start + WP])
            if start != d * W:
                moved = pltpu.roll(moved, WP - (d * W - start), 1)
            moved = jnp.where(lane < W, moved, extra).astype(BF)
            for y in range(Y):
                out_ref[y * G + d, t * G : (t + 1) * G, :] = moved


def pack(me, counts, dest, tokens, cotangent):
    return pl.pallas_call(
        pack_kernel,
        out_shape=jax.ShapeDtypeStruct((Y * G, 2 * G, WP), BF),
        in_specs=[SMEM, SMEM, VMEM, VMEM, VMEM],
        out_specs=VMEM,
        name="pack",
    )(me, counts, dest, tokens, cotangent)


def rows_kernel(own_ref, other_ref, x_ref, xt_ref):
    lane = lax.broadcasted_iota(jnp.int32, (G, 128), 1)
    for n in range(N):
        recv_ref = (own_ref, other_ref)[n // Y]
        first_block = n % Y * G
        table = jnp.zeros((G, 128), F32)
        for g in range(G):
            table = table + recv_ref[first_block + g, 0:G, WP - 128 : WP].astype(F32)
        for e in range(E):
            kept = jnp.sum(jnp.where(lane == 128 - (WP - W) + e, table, 0.0), axis=1, keepdims=True)
            kept = jnp.broadcast_to(kept, (G, W))
            for c in range(C):
                at = n * Q + c * G
                for t in range(2):
                    block = recv_ref[first_block + e * C + c, t * G : (t + 1) * G, 0:W].astype(F32)
                    x_ref[t, e, at : at + G, :] = jnp.where(kept > c + 0.5, block, 0.0).astype(BF)
    for t in range(2):
        for e in range(E):
            xt_ref[t, e] = x_ref[t, e].astype(F32).T.astype(BF)


def prepare(own, other):
    return pl.pallas_call(
        rows_kernel,
        out_shape=(jax.ShapeDtypeStruct((2, E, R, W), BF), jax.ShapeDtypeStruct((2, E, W, R), BF)),
        in_specs=[VMEM, VMEM],
        out_specs=(VMEM, VMEM),
        compiler_params=pltpu.CompilerParams(vmem_limit_bytes=LIMIT),
        name="prepare",
    )(own, other)


def first_kernel(expert_ref, half_ref, x_ref, weight_ref, out_ref):
    rows = pl.ds(pl.multiple_of(half_ref[0] * H, H), H)
    for i in range(Z // 2):
        e = expert_ref[Z // 2 * pl.program_id(0) + i]
        both = jnp.concatenate([weight_ref[i, 0], weight_ref[i, 1]], axis=1)
        out_ref[i, :, 0 : 2 * S] = dot(x_ref[0, e, rows, :], both).astype(out_ref.dtype)
        out_ref[i, :, 2 * S : 3 * S] = dot(x_ref[1, e, rows, :], weight_ref[i, 2]).astype(out_ref.dtype)


def first(expert, half, x, weight, dtype):
    return pl.pallas_call(
        first_kernel,
        out_shape=jax.ShapeDtypeStruct((Z, H, 3 * S), dtype),
        grid=(2,),
        in_specs=[SMEM, SMEM, VMEM, pl.BlockSpec((Z // 2, 3, W, S), lambda i: (i, 0, 0, 0))],
        out_specs=pl.BlockSpec((Z // 2, H, 3 * S), lambda i: (i, 0, 0)),
        compiler_params=pltpu.CompilerParams(vmem_limit_bytes=LIMIT),
        name="first",
    )(expert, half, x, weight)


def add_kernel(keep_ref, got_ref, out_ref):
    for z in range(Z):
        out_ref[z] = (keep_ref[z] + got_ref[z].astype(F32)).astype(BF)


def add_cores(keep, got):
    return pl.pallas_call(
        add_kernel,
        out_shape=jax.ShapeDtypeStruct((Z, H, 3 * S), BF),
        in_specs=[VMEM, VMEM],
        out_specs=VMEM,
        compiler_params=pltpu.CompilerParams(vmem_limit_bytes=LIMIT),
        name="add_cores",
    )(keep, got)


def middle_kernel(part_ref, out_ref):
    total = part_ref[0].astype(F32)
    for d in range(1, Z):
        total = total + part_ref[d].astype(F32)
    gate = total[:, 0:S]
    up = total[:, S : 2 * S]
    hidden_grad = total[:, 2 * S : 3 * S]
    sigmoid = jax.nn.sigmoid(gate)
    activated = gate * sigmoid
    hidden = (activated * up).astype(BF)
    gate_grad = (hidden_grad * up * sigmoid * (1.0 + gate * (1.0 - sigmoid))).astype(BF)
    up_grad = (hidden_grad * activated).astype(BF)
    for d in range(Z):
        out_ref[d, :, 0:S] = hidden
        out_ref[d, :, S : 2 * S] = gate_grad
        out_ref[d, :, 2 * S : 3 * S] = up_grad


def middle(parts):
    block = pl.BlockSpec((Z, H // 2, 3 * S), lambda i: (0, i, 0))
    return pl.pallas_call(
        middle_kernel,
        grid=(2,),
        out_shape=jax.ShapeDtypeStruct((Z, H, 3 * S), BF),
        in_specs=[block],
        out_specs=block,
        compiler_params=pltpu.CompilerParams(vmem_limit_bytes=LIMIT),
        name="middle",
    )(parts)


def in_order(core, mine, other):
    low = jnp.broadcast_to(core, mine.shape) == 0
    return jnp.concatenate([jnp.where(low, mine, other), jnp.where(low, other, mine)], axis=0)


def weigh_kernel(expert_ref, core_ref, xt_ref, mine_ref, other_ref, out_ref, held_ref, sems):
    copies = [pltpu.make_async_copy(held_ref.at[z], out_ref.at[z], sems.at[z]) for z in range(Z)]
    for z in range(Z):
        e = expert_ref[z]
        act = in_order(core_ref[0], mine_ref[z], other_ref[z])
        both = dot(xt_ref[0, e], act[:, S : 3 * S])
        held_ref[z, 0] = both[:, 0:S].astype(BF)
        held_ref[z, 1] = both[:, S : 2 * S].astype(BF)
        held_ref[z, 2] = dot(xt_ref[1, e], act[:, 0:S]).astype(BF)
        copies[z].start()
    for copy in copies:
        copy.wait()


def weigh(expert, core, xt, mine, other):
    return pl.pallas_call(
        weigh_kernel,
        out_shape=pltpu.HBM((Z, 3, W, S), BF),
        in_specs=[SMEM, SMEM, VMEM, VMEM, VMEM],
        out_specs=pl.BlockSpec(memory_space=pl.ANY),
        scratch_shapes=[pltpu.VMEM((Z, 3, W, S), BF), pltpu.SemaphoreType.DMA((Z,))],
        compiler_params=pltpu.CompilerParams(vmem_limit_bytes=LIMIT),
        name="weigh",
    )(expert, core, xt, mine, other)


def last_kernel(expert_ref, core_ref, weight_ref, mine_ref, far_ref, own_ref, other_ref, acc_ref):
    acc_ref[...] = jnp.zeros_like(acc_ref)
    tail = ((1,), (1,))

    def step(z, carry):
        e = expert_ref[z]
        act = in_order(core_ref[0], mine_ref[z], far_ref[z])
        acc_ref[0, e] += dot(act[:, 0:S], weight_ref[z, 2], tail)
        both = jnp.concatenate([weight_ref[z, 0], weight_ref[z, 1]], axis=1)
        acc_ref[1, e] += dot(act[:, S : 3 * S], both, tail)
        return carry

    lax.fori_loop(0, Z, step, 0)
    size = E * Q
    i = lax.broadcasted_iota(jnp.int32, (size, size), 0)
    j = lax.broadcasted_iota(jnp.int32, (size, size), 1)
    swap = ((i // (E * C) == j % G) & (i % (E * C) == j // G)).astype(F32).astype(BF)
    for n in range(N):
        out_ref = (own_ref, other_ref)[n // Y]
        first_block = n % Y * G
        for t in range(2):
            rows = jnp.concatenate([acc_ref[t, e, n * Q : (n + 1) * Q, :].astype(BF) for e in range(E)], axis=0)
            moved = dot(swap, rows).astype(BF)
            for h in range(G):
                out_ref[first_block + h, t * G : (t + 1) * G, 0:W] = moved[h * E * C : (h + 1) * E * C, :]
                out_ref[first_block + h, t * G : (t + 1) * G, W:WP] = jnp.zeros((E * C, WP - W), BF)


def last(expert, core, weight, mine, far):
    shape = jax.ShapeDtypeStruct((Y * G, 2 * G, WP), BF)
    return pl.pallas_call(
        last_kernel,
        out_shape=(shape, shape),
        in_specs=[SMEM, SMEM, VMEM, VMEM, VMEM],
        out_specs=(VMEM, VMEM),
        scratch_shapes=[pltpu.VMEM((2, E, R, W), F32)],
        compiler_params=pltpu.CompilerParams(vmem_limit_bytes=LIMIT),
        name="last",
    )(expert, core, weight, mine, far)


def unpack_rows(recv_ref, t):
    low = lax.broadcasted_iota(jnp.int32, (G, 128), 1) < W - 256
    rows = slice(t * G, (t + 1) * G)
    for d in range(0, G, 2):
        left = recv_ref[d, rows, :].astype(F32) + recv_ref[G + d, rows, :].astype(F32)
        right = recv_ref[d + 1, rows, :].astype(F32) + recv_ref[G + d + 1, rows, :].astype(F32)
        right = pltpu.roll(right, W - 256, 1)
        yield slice(d * W, d * W + 256), left[:, 0:256]
        yield slice(d * W + 256, d * W + 384), jnp.where(low, left[:, 256:384], right[:, 0:128])
        yield slice(d * W + 384, d * W + 640), right[:, 128:384]


def unpack_other_kernel(recv_ref, out_ref):
    for t in range(2):
        for at, part in unpack_rows(recv_ref, t):
            out_ref[t, :, at] = part.astype(BF)


def unpack_other(recv):
    return pl.pallas_call(
        unpack_other_kernel,
        out_shape=jax.ShapeDtypeStruct((2, E * C, D), BF),
        in_specs=[VMEM],
        out_specs=VMEM,
        compiler_params=pltpu.CompilerParams(vmem_limit_bytes=LIMIT),
        name="unpack_other",
    )(recv)


def unpack_own_kernel(recv_ref, add_ref, layer_ref, grad_ref):
    for t, ref in enumerate((layer_ref, grad_ref)):
        for at, part in unpack_rows(recv_ref, t):
            ref[:, at] = (part + add_ref[t, :, at].astype(F32)).astype(BF)


def unpack_own(recv, add):
    shape = jax.ShapeDtypeStruct((E * C, D), BF)
    return pl.pallas_call(
        unpack_own_kernel,
        out_shape=(shape, shape),
        in_specs=[VMEM, VMEM],
        out_specs=(VMEM, VMEM),
        compiler_params=pltpu.CompilerParams(vmem_limit_bytes=LIMIT),
        name="unpack_own",
    )(recv, add)


def widen_kernel(own_ref, gate_up_ref, down_ref):
    gate_up_ref[0] = own_ref[0, 0:2].astype(F32)
    down_ref[0] = own_ref[0, 2].astype(F32)


def widen(own):
    return pl.pallas_call(
        widen_kernel,
        out_shape=(jax.ShapeDtypeStruct((1, 2, W, S), F32), jax.ShapeDtypeStruct((1, W, S), F32)),
        in_specs=[VMEM],
        out_specs=(VMEM, VMEM),
        name="widen",
    )(own)


def exchange(x, axes):
    return lax.all_to_all(x, axes, split_axis=0, concat_axis=0, tiled=True)


def gather(x):
    return lax.all_gather(x, "z_hi", axis=0, tiled=True)


def scatter(x):
    return lax.psum_scatter(x, "z_hi", scatter_dimension=0, tiled=True)


def swap(*xs, axis="z_lo"):
    return [lax.ppermute(x, axis, ((0, 1), (1, 0))) for x in xs]


def swap_cores(x):
    return swap(x, axis="core")[0]


def body(tokens, cotangent, counts, destination, placement, gate_up_weight, down_weight):
    local = jnp.concatenate([gate_up_weight, down_weight[:, None]], axis=1)
    weight = gather(local)
    me = lax.axis_index(GRP).reshape(1).astype(jnp.int32)
    near = lax.dynamic_index_in_dim(placement.reshape(Z, N), lax.axis_index(NEAR), 1, keepdims=False)
    expert = near // (Z * N // E)
    rows = jnp.concatenate([tokens, cotangent], axis=0)
    table = jnp.concatenate([counts[0, 0], destination[0, 0]])[None]
    far_table, far_rows = swap(table, rows)
    sent = pack(me, counts[0, 0], destination[0], tokens[0], cotangent[0])
    own = exchange(sent, PLANE)
    sent = pack(me, far_table[0, 0:E], far_table[:, E:], far_rows[0], far_rows[1])
    other = exchange(sent, PLANE)
    x, xt = prepare(own, other)
    core = lax.axis_index("core").reshape(1).astype(jnp.int32)
    streamed = pltpu.with_memory_space_constraint(weight, pltpu.HBM)
    got = swap_cores(first(expert, 1 - core, x, streamed, BF))
    keep = first(expert, core, x, weight, F32)
    parts = add_cores(keep, got)
    act = middle(exchange(parts, CHIPS))
    mine = exchange(act, CHIPS)
    far = swap_cores(mine)
    reduced = scatter(weigh(expert, core, xt, mine, far))
    own, other = last(expert, core, weight, mine, far)
    other = unpack_other(exchange(other, PLANE))
    (other,) = swap(other)
    layer_out, input_grad = unpack_own(exchange(own, PLANE), other)
    gate_up_grad, down_grad = widen(reduced)
    return (layer_out[None], input_grad[None], gate_up_grad, down_grad)


def solution(mesh):
    fine = Mesh(mesh.devices.reshape(SIZES), AXES)
    return jax.shard_map(
        body,
        mesh=fine,
        in_specs=(
            P(GRP, EP, None),
            P(GRP, EP, None),
            P(GRP, EP, None),
            P(GRP, EP, None),
            P(),
            P(EP, None, GRP, None),
            P(EP, GRP, None),
        ),
        out_specs=(
            P(GRP, EP, None),
            P(GRP, EP, None),
            P(EP, None, GRP, None),
            P(EP, GRP, None),
        ),
        check_vma=False,
    )
```

```python
import jax
import jax.numpy as jnp
from jax import lax
from jax.experimental import pallas as pl
from jax.experimental.pallas import tpu as pltpu
from jax.sharding import Mesh, PartitionSpec as P


AXES = ("y_lo", "x", "core", "z_hi", "z_lo", "y_hi")
SIZES = (2, 4, 2, 8, 2, 2)
GRP = ("y_lo", "x", "core")
EP = ("z_hi", "z_lo", "y_hi")
NEAR = ("z_lo", "y_hi")
PLANE = ("y_hi",) + GRP

G = 16
Z = 8
Y = 2
N = 2 * Y
E = 4
C = 4
D = 5120
W = D // G
WP = 384
S = 128
Q = C * G
R = N * Q
CHIPS = ("y_lo", "x")
H = R // 2
BF = jnp.bfloat16
F32 = jnp.float32
LIMIT = 24 << 20
VMEM = pl.BlockSpec(memory_space=pltpu.VMEM)
SMEM = pl.BlockSpec(memory_space=pltpu.SMEM)


def dot(a, b, dims=((1,), (0,))):
    return lax.dot_general(a, b, (dims, ((), ())), preferred_element_type=F32)


def pack_kernel(me_ref, counts_ref, dest_ref, tok_ref, cot_ref, out_ref):
    me = me_ref[0]
    rows = lax.broadcasted_iota(jnp.int32, (G, G), 0)
    pick = (rows == dest_ref[...]).astype(F32).astype(BF)
    lane = lax.broadcasted_iota(jnp.int32, (G, WP), 1)
    row = lax.broadcasted_iota(jnp.int32, (G, WP), 0)
    extra = jnp.zeros((G, WP), F32)
    for e in range(E):
        extra = jnp.where((lane == W + e) & (row == me), counts_ref[e].astype(F32), extra)
    for d in range(G):
        start = d * W // 128 * 128
        for t, ref in enumerate((tok_ref, cot_ref)):
            moved = dot(pick, ref[:, start : start + WP])
            if start != d * W:
                moved = pltpu.roll(moved, WP - (d * W - start), 1)
            moved = jnp.where(lane < W, moved, extra).astype(BF)
            for y in range(Y):
                out_ref[y * G + d, t * G : (t + 1) * G, :] = moved


def pack(me, counts, dest, tokens, cotangent):
    return pl.pallas_call(
        pack_kernel,
        out_shape=jax.ShapeDtypeStruct((Y * G, 2 * G, WP), BF),
        in_specs=[SMEM, SMEM, VMEM, VMEM, VMEM],
        out_specs=VMEM,
        name="pack",
    )(me, counts, dest, tokens, cotangent)


def rows_kernel(own_ref, other_ref, x_ref, xt_ref):
    lane = lax.broadcasted_iota(jnp.int32, (G, 128), 1)
    for n in range(N):
        recv_ref = (own_ref, other_ref)[n // Y]
        first_block = n % Y * G
        table = jnp.zeros((G, 128), F32)
        for g in range(G):
            table = table + recv_ref[first_block + g, 0:G, WP - 128 : WP].astype(F32)
        for e in range(E):
            kept = jnp.sum(jnp.where(lane == 128 - (WP - W) + e, table, 0.0), axis=1, keepdims=True)
            kept = jnp.broadcast_to(kept, (G, W))
            for c in range(C):
                at = n * Q + c * G
                for t in range(2):
                    block = recv_ref[first_block + e * C + c, t * G : (t + 1) * G, 0:W].astype(F32)
                    x_ref[t, e, at : at + G, :] = jnp.where(kept > c + 0.5, block, 0.0).astype(BF)
    for t in range(2):
        for e in range(E):
            xt_ref[t, e] = x_ref[t, e].astype(F32).T.astype(BF)


def prepare(own, other):
    return pl.pallas_call(
        rows_kernel,
        out_shape=(jax.ShapeDtypeStruct((2, E, R, W), BF), jax.ShapeDtypeStruct((2, E, W, R), BF)),
        in_specs=[VMEM, VMEM],
        out_specs=(VMEM, VMEM),
        compiler_params=pltpu.CompilerParams(vmem_limit_bytes=LIMIT),
        name="prepare",
    )(own, other)


def first_kernel(expert_ref, half_ref, x_ref, weight_ref, out_ref):
    rows = pl.ds(pl.multiple_of(half_ref[0] * H, H), H)
    for i in range(Z // 2):
        e = expert_ref[Z // 2 * pl.program_id(0) + i]
        both = jnp.concatenate([weight_ref[i, 0], weight_ref[i, 1]], axis=1)
        out_ref[i, :, 0 : 2 * S] = dot(x_ref[0, e, rows, :], both).astype(out_ref.dtype)
        out_ref[i, :, 2 * S : 3 * S] = dot(x_ref[1, e, rows, :], weight_ref[i, 2]).astype(out_ref.dtype)


def first(expert, half, x, weight, dtype):
    return pl.pallas_call(
        first_kernel,
        out_shape=jax.ShapeDtypeStruct((Z, H, 3 * S), dtype),
        grid=(2,),
        in_specs=[SMEM, SMEM, VMEM, pl.BlockSpec((Z // 2, 3, W, S), lambda i: (i, 0, 0, 0))],
        out_specs=pl.BlockSpec((Z // 2, H, 3 * S), lambda i: (i, 0, 0)),
        compiler_params=pltpu.CompilerParams(vmem_limit_bytes=LIMIT),
        name="first",
    )(expert, half, x, weight)


def add_kernel(keep_ref, got_ref, out_ref):
    for z in range(Z):
        out_ref[z] = (keep_ref[z] + got_ref[z].astype(F32)).astype(BF)


def add_cores(keep, got):
    return pl.pallas_call(
        add_kernel,
        out_shape=jax.ShapeDtypeStruct((Z, H, 3 * S), BF),
        in_specs=[VMEM, VMEM],
        out_specs=VMEM,
        compiler_params=pltpu.CompilerParams(vmem_limit_bytes=LIMIT),
        name="add_cores",
    )(keep, got)


def middle_kernel(part_ref, out_ref):
    total = part_ref[0].astype(F32)
    for d in range(1, Z):
        total = total + part_ref[d].astype(F32)
    gate = total[:, 0:S]
    up = total[:, S : 2 * S]
    hidden_grad = total[:, 2 * S : 3 * S]
    sigmoid = jax.nn.sigmoid(gate)
    activated = gate * sigmoid
    hidden = (activated * up).astype(BF)
    gate_grad = (hidden_grad * up * sigmoid * (1.0 + gate * (1.0 - sigmoid))).astype(BF)
    up_grad = (hidden_grad * activated).astype(BF)
    for d in range(Z):
        out_ref[d, :, 0:S] = hidden
        out_ref[d, :, S : 2 * S] = gate_grad
        out_ref[d, :, 2 * S : 3 * S] = up_grad


def middle(parts):
    block = pl.BlockSpec((Z, H // 2, 3 * S), lambda i: (0, i, 0))
    return pl.pallas_call(
        middle_kernel,
        grid=(2,),
        out_shape=jax.ShapeDtypeStruct((Z, H, 3 * S), BF),
        in_specs=[block],
        out_specs=block,
        compiler_params=pltpu.CompilerParams(vmem_limit_bytes=LIMIT),
        name="middle",
    )(parts)


def in_order(core, mine, other):
    low = jnp.broadcast_to(core, mine.shape) == 0
    return jnp.concatenate([jnp.where(low, mine, other), jnp.where(low, other, mine)], axis=0)


def weigh_kernel(expert_ref, core_ref, xt_ref, mine_ref, other_ref, out_ref, held_ref, sems):
    copies = [pltpu.make_async_copy(held_ref.at[z], out_ref.at[z], sems.at[z]) for z in range(Z)]
    for z in range(Z):
        e = expert_ref[z]
        act = in_order(core_ref[0], mine_ref[z], other_ref[z])
        both = dot(xt_ref[0, e], act[:, S : 3 * S])
        held_ref[z, 0] = both[:, 0:S].astype(BF)
        held_ref[z, 1] = both[:, S : 2 * S].astype(BF)
        held_ref[z, 2] = dot(xt_ref[1, e], act[:, 0:S]).astype(BF)
        copies[z].start()
    for copy in copies:
        copy.wait()


def weigh(expert, core, xt, mine, other):
    return pl.pallas_call(
        weigh_kernel,
        out_shape=pltpu.HBM((Z, 3, W, S), BF),
        in_specs=[SMEM, SMEM, VMEM, VMEM, VMEM],
        out_specs=pl.BlockSpec(memory_space=pl.ANY),
        scratch_shapes=[pltpu.VMEM((Z, 3, W, S), BF), pltpu.SemaphoreType.DMA((Z,))],
        compiler_params=pltpu.CompilerParams(vmem_limit_bytes=LIMIT),
        name="weigh",
    )(expert, core, xt, mine, other)


def last_kernel(expert_ref, core_ref, weight_ref, mine_ref, far_ref, own_ref, other_ref, acc_ref):
    acc_ref[...] = jnp.zeros_like(acc_ref)
    tail = ((1,), (1,))

    def step(z, carry):
        e = expert_ref[z]
        act = in_order(core_ref[0], mine_ref[z], far_ref[z])
        acc_ref[0, e] += dot(act[:, 0:S], weight_ref[z, 2], tail)
        both = jnp.concatenate([weight_ref[z, 0], weight_ref[z, 1]], axis=1)
        acc_ref[1, e] += dot(act[:, S : 3 * S], both, tail)
        return carry

    lax.fori_loop(0, Z, step, 0)
    size = E * Q
    i = lax.broadcasted_iota(jnp.int32, (size, size), 0)
    j = lax.broadcasted_iota(jnp.int32, (size, size), 1)
    swap = ((i // (E * C) == j % G) & (i % (E * C) == j // G)).astype(F32).astype(BF)
    for n in range(N):
        out_ref = (own_ref, other_ref)[n // Y]
        first_block = n % Y * G
        for t in range(2):
            rows = jnp.concatenate([acc_ref[t, e, n * Q : (n + 1) * Q, :].astype(BF) for e in range(E)], axis=0)
            moved = dot(swap, rows).astype(BF)
            for h in range(G):
                out_ref[first_block + h, t * G : (t + 1) * G, 0:W] = moved[h * E * C : (h + 1) * E * C, :]
                out_ref[first_block + h, t * G : (t + 1) * G, W:WP] = jnp.zeros((E * C, WP - W), BF)


def last(expert, core, weight, mine, far):
    shape = jax.ShapeDtypeStruct((Y * G, 2 * G, WP), BF)
    return pl.pallas_call(
        last_kernel,
        out_shape=(shape, shape),
        in_specs=[SMEM, SMEM, VMEM, VMEM, VMEM],
        out_specs=(VMEM, VMEM),
        scratch_shapes=[pltpu.VMEM((2, E, R, W), F32)],
        compiler_params=pltpu.CompilerParams(vmem_limit_bytes=LIMIT),
        name="last",
    )(expert, core, weight, mine, far)


def unpack_rows(recv_ref, t):
    low = lax.broadcasted_iota(jnp.int32, (G, 128), 1) < W - 256
    rows = slice(t * G, (t + 1) * G)
    for d in range(0, G, 2):
        left = recv_ref[d, rows, :].astype(F32) + recv_ref[G + d, rows, :].astype(F32)
        right = recv_ref[d + 1, rows, :].astype(F32) + recv_ref[G + d + 1, rows, :].astype(F32)
        right = pltpu.roll(right, W - 256, 1)
        yield slice(d * W, d * W + 256), left[:, 0:256]
        yield slice(d * W + 256, d * W + 384), jnp.where(low, left[:, 256:384], right[:, 0:128])
        yield slice(d * W + 384, d * W + 640), right[:, 128:384]


def unpack_other_kernel(recv_ref, out_ref):
    for t in range(2):
        for at, part in unpack_rows(recv_ref, t):
            out_ref[t, :, at] = part.astype(BF)


def unpack_other(recv):
    return pl.pallas_call(
        unpack_other_kernel,
        out_shape=jax.ShapeDtypeStruct((2, E * C, D), BF),
        in_specs=[VMEM],
        out_specs=VMEM,
        compiler_params=pltpu.CompilerParams(vmem_limit_bytes=LIMIT),
        name="unpack_other",
    )(recv)


def unpack_own_kernel(recv_ref, add_ref, layer_ref, grad_ref):
    for t, ref in enumerate((layer_ref, grad_ref)):
        for at, part in unpack_rows(recv_ref, t):
            ref[:, at] = (part + add_ref[t, :, at].astype(F32)).astype(BF)


def unpack_own(recv, add):
    shape = jax.ShapeDtypeStruct((E * C, D), BF)
    return pl.pallas_call(
        unpack_own_kernel,
        out_shape=(shape, shape),
        in_specs=[VMEM, VMEM],
        out_specs=(VMEM, VMEM),
        compiler_params=pltpu.CompilerParams(vmem_limit_bytes=LIMIT),
        name="unpack_own",
    )(recv, add)


def widen_kernel(own_ref, gate_up_ref, down_ref):
    gate_up_ref[0] = own_ref[0, 0:2].astype(F32)
    down_ref[0] = own_ref[0, 2].astype(F32)


def widen(own):
    return pl.pallas_call(
        widen_kernel,
        out_shape=(jax.ShapeDtypeStruct((1, 2, W, S), F32), jax.ShapeDtypeStruct((1, W, S), F32)),
        in_specs=[VMEM],
        out_specs=(VMEM, VMEM),
        name="widen",
    )(own)


def exchange(x, axes):
    return lax.all_to_all(x, axes, split_axis=0, concat_axis=0, tiled=True)


def gather(x):
    return lax.all_gather(x.reshape(3 * W, S), "z_hi", axis=0, tiled=True).reshape(Z, 3, W, S)


def scatter(x):
    flat = x.reshape(Z * 3 * W, S)
    return lax.psum_scatter(flat, "z_hi", scatter_dimension=0, tiled=True).reshape(1, 3, W, S)


def swap(*xs, axis="z_lo"):
    return [lax.ppermute(x, axis, ((0, 1), (1, 0))) for x in xs]


def swap_cores(x):
    return swap(x, axis="core")[0]


def body(tokens, cotangent, counts, destination, placement, gate_up_weight, down_weight):
    local = jnp.concatenate([gate_up_weight, down_weight[:, None]], axis=1)
    weight = gather(local)
    me = lax.axis_index(GRP).reshape(1).astype(jnp.int32)
    near = lax.dynamic_index_in_dim(placement.reshape(Z, N), lax.axis_index(NEAR), 1, keepdims=False)
    expert = near // (Z * N // E)
    rows = jnp.concatenate([tokens, cotangent], axis=0)
    table = jnp.concatenate([counts[0, 0], destination[0, 0]])[None]
    far_table, far_rows = swap(table, rows)
    sent = pack(me, counts[0, 0], destination[0], tokens[0], cotangent[0])
    own = exchange(sent, PLANE)
    sent = pack(me, far_table[0, 0:E], far_table[:, E:], far_rows[0], far_rows[1])
    other = exchange(sent, PLANE)
    x, xt = prepare(own, other)
    core = lax.axis_index("core").reshape(1).astype(jnp.int32)
    streamed = pltpu.with_memory_space_constraint(weight, pltpu.HBM)
    got = swap_cores(first(expert, 1 - core, x, streamed, BF))
    keep = first(expert, core, x, weight, F32)
    parts = add_cores(keep, got)
    act = middle(exchange(parts, CHIPS))
    mine = exchange(act, CHIPS)
    far = swap_cores(mine)
    reduced = scatter(weigh(expert, core, xt, mine, far))
    own, other = last(expert, core, weight, mine, far)
    other = unpack_other(exchange(other, PLANE))
    (other,) = swap(other)
    layer_out, input_grad = unpack_own(exchange(own, PLANE), other)
    gate_up_grad, down_grad = widen(reduced)
    return (layer_out[None], input_grad[None], gate_up_grad, down_grad)


def solution(mesh):
    fine = Mesh(mesh.devices.reshape(SIZES), AXES)
    return jax.shard_map(
        body,
        mesh=fine,
        in_specs=(
            P(GRP, EP, None),
            P(GRP, EP, None),
            P(GRP, EP, None),
            P(GRP, EP, None),
            P(),
            P(EP, None, GRP, None),
            P(EP, GRP, None),
        ),
        out_specs=(
            P(GRP, EP, None),
            P(GRP, EP, None),
            P(EP, None, GRP, None),
            P(EP, GRP, None),
        ),
        check_vma=False,
    )
```
